512 devices in a mesh: grp: 8 (over y_lo, x), sub: 64 (over z, y_hi, core).
Axes of the slice: x: 4, y: 8 (y_hi: 4, y_lo: 2; y = y_hi * 2 + y_lo), z: 8, core: 2. Of those that a mesh axis runs over, the one named last changes fastest.
Arguments:
- schur_t: bfloat16 [8, 64, 1024, 1024], P('grp', 'sub')
- neumann_t: bfloat16 [8, 64, 1024, 1024], P('grp', 'sub')
- face_weights: float32 [8, 64, 1024], P('grp', 'sub'), as said below
- coarse_basis: bfloat16 [8, 64, 1024, 24], P('grp', 'sub'), may hold values from -0.375 to 0.375
- coarse_inverse: float32 [8, 768, 768], P('grp', 'sub')
- coarse_number: int32 [8, 1536], P('grp'), may hold values from 0 to 767, as said below
- loads: bfloat16 [8, 64, 1024, 128], P('grp', 'sub'), may hold values from -6 to 6
- iterate: bfloat16 [8, 64, 1024, 128], P('grp', 'sub'), as said below
Outputs:
- iterate_out: bfloat16 [8, 64, 1024, 128], P('grp', 'sub')
The draws below stay inside these ranges and needn't reach their ends.
Inputs may be any that keep to these rules, and one draw needn't show every extreme that they name: `face_weights`: the weights of an unknown and of its partner unknown on the face it shares sum to one. `coarse_number`: each value appears exactly twice in each group's row. `iterate`: equal on the two copies of each shared unknown.
All inputs are finite; a program needn't handle non-finite values.
Results may differ from the reference program's by a relative error of at most 0.0051.
Values sent between devices are 32-bit elements; how exact they have to be, the bound alone decides.
A program may use at most 64 MiB of HBM per device.

```python
import math
import jax
import jax.numpy as jnp
from jax import lax

IFACE = 1024
RHS = 128
NCL = 24
NC = 768
ITERS = 3
N_GRP = 8
N_SUB = 64


def diagonal_helper(key):
    inner = jax.random.fold_in(key, 11)
    shape = (N_GRP, N_SUB, IFACE)
    values = jnp.exp(jax.random.uniform(inner, shape, jnp.float32, 0.0, math.log(4.0)))
    return values


def spread_helper(key, shape):
    return jax.random.normal(key, shape, jnp.float32)


def draw_schur_t(key, part):
    diagonal = diagonal_helper(key)
    shape = (N_GRP, N_SUB, IFACE, IFACE)
    off = spread_helper(jax.random.fold_in(key, 12), shape) * (0.7 / math.sqrt(IFACE))
    identity = jnp.eye(IFACE, dtype=jnp.float32)
    return (off + diagonal[..., None] * identity).astype(jnp.bfloat16)


def draw_neumann_t(key, part):
    diagonal = diagonal_helper(key)
    shape = (N_GRP, N_SUB, IFACE, IFACE)
    off = spread_helper(jax.random.fold_in(key, 13), shape) * (0.3 / math.sqrt(IFACE))
    identity = jnp.eye(IFACE, dtype=jnp.float32)
    return (off + (1.0 / diagonal)[..., None] * identity).astype(jnp.bfloat16)


def draw_face_weights(key, part):
    diagonal = diagonal_helper(key).reshape(N_GRP, N_SUB, 4, IFACE // 4)
    first = jnp.roll(diagonal[:, :, 1], 1, axis=1)
    second = jnp.roll(diagonal[:, :, 0], -1, axis=1)
    third = jnp.roll(diagonal[:, :, 3], 1, axis=0)
    fourth = jnp.roll(diagonal[:, :, 2], -1, axis=0)
    mates = jnp.stack([first, second, third, fourth], axis=2)
    return (diagonal / (diagonal + mates)).reshape(N_GRP, N_SUB, IFACE).astype(jnp.float32)


def draw_coarse_inverse(key, part):
    shape = (N_GRP, NC)
    inner = jax.random.fold_in(key, 21)
    diagonal = jnp.exp(jax.random.uniform(inner, shape, jnp.float32, math.log(0.5), math.log(2.0)))
    off = spread_helper(jax.random.fold_in(key, 22), (N_GRP, NC, NC)) * (0.4 / math.sqrt(NC))
    identity = jnp.eye(NC, dtype=jnp.float32)
    return (off + diagonal[..., None] * identity).astype(jnp.float32)


def draw_coarse_number(key, part):
    keys = jax.random.split(jax.random.fold_in(key, 31), N_GRP)
    orders = jax.vmap(lambda k: jax.random.permutation(k, N_SUB * NCL))(keys)
    return (orders % NC).astype(jnp.int32)


def draw_iterate(key, part):
    shape = (N_GRP, N_SUB, 4, IFACE // 4, RHS)
    values = spread_helper(jax.random.fold_in(key, 41), shape)
    second = jnp.roll(values[:, :, 0], -1, axis=1)
    fourth = jnp.roll(values[:, :, 2], -1, axis=0)
    joined = jnp.stack([values[:, :, 0], second, values[:, :, 2], fourth], axis=2)
    return joined.reshape(N_GRP, N_SUB, IFACE, RHS).astype(jnp.bfloat16)


def level_of(own_key, dims, shards, smallest, high):
    level, own = 1.0, jax.random.fold_in(own_key, 6)
    for axis_at, shards_of in shards:
        heights = jnp.exp(jax.random.uniform(jax.random.fold_in(own, axis_at), (shards_of,), jnp.float32, smallest / len(shards), high / len(shards)))
        level = level * jnp.repeat(heights, dims[axis_at] // shards_of).reshape([-1 if axis == axis_at else 1 for axis in range(len(dims))])
    return level


def scatter_about(own_key, extent, width, most, pieces=(), kind=jnp.bfloat16):
    values = width * jax.random.normal(own_key, extent, jnp.float32)
    if pieces:
        values = values * level_of(own_key, extent, pieces, -0.22, 0.18)
    return jnp.clip(values, -most, most).astype(kind)


def setup_inputs(seed: int = 0) -> dict:
    streams_of = jax.random.split(jax.random.key(seed), 9)
    return {
        "schur_t": draw_schur_t(jax.random.fold_in(streams_of[8], 71), 0),
        "neumann_t": draw_neumann_t(jax.random.fold_in(streams_of[8], 71), 0),
        "face_weights": draw_face_weights(jax.random.fold_in(streams_of[8], 71), 0),
        "coarse_basis": scatter_about(streams_of[3], (N_GRP, N_SUB, IFACE, NCL), (IFACE // 4) ** -0.5, 0.375, ((0, 8), (1, 64))),
        "coarse_inverse": draw_coarse_inverse(jax.random.fold_in(streams_of[8], 71), 0),
        "coarse_number": draw_coarse_number(jax.random.fold_in(streams_of[8], 71), 0),
        "loads": scatter_about(streams_of[6], (N_GRP, N_SUB, IFACE, RHS), 1.0, 6.0, ((0, 8), (1, 64))),
        "iterate": draw_iterate(jax.random.fold_in(streams_of[8], 71), 0),
    }


def partner(values):
    columns = values.shape[-1]
    faces = values.reshape(N_GRP, N_SUB, 4, IFACE // 4, columns)
    first = jnp.roll(faces[:, :, 1], 1, axis=1)
    second = jnp.roll(faces[:, :, 0], -1, axis=1)
    third = jnp.roll(faces[:, :, 3], 1, axis=0)
    fourth = jnp.roll(faces[:, :, 2], -1, axis=0)
    return jnp.stack([first, second, third, fourth], axis=2).reshape(N_GRP, N_SUB, IFACE, columns)


def products(mats, vectors):
    return lax.map(lambda pair: jnp.dot(pair[0], pair[1], preferred_element_type=jnp.float32), (mats, vectors))


def reference(schur_t, neumann_t, face_weights, coarse_basis, coarse_inverse, coarse_number, loads, iterate):
    whole = (N_GRP, N_SUB, IFACE, RHS)
    flat = (N_GRP * N_SUB, IFACE, RHS)
    schur_flat = schur_t.reshape(N_GRP * N_SUB, IFACE, IFACE)
    neumann_flat = neumann_t.reshape(N_GRP * N_SUB, IFACE, IFACE)
    weights = face_weights[..., None]
    basis_wide = coarse_basis.astype(jnp.float32)
    load_wide = loads.astype(jnp.float32)
    highest = lax.Precision.HIGHEST
    current = iterate
    for step in range(ITERS):
        image = products(schur_flat, current.reshape(flat)).reshape(whole)
        part = load_wide - image
        resid = part + partner(part)
        weighted = (weights * resid).astype(jnp.bfloat16)
        local_coarse = jnp.einsum("gsin,gsik->gsnk", basis_wide, weighted.astype(jnp.float32), precision=highest)
        coarse_rhs = jax.vmap(lambda c, n: jax.ops.segment_sum(c, n, num_segments=NC))(
            local_coarse.reshape(N_GRP, N_SUB * NCL, RHS), coarse_number)
        solved = jnp.einsum("gnm,gmk->gnk", coarse_inverse, coarse_rhs, precision=highest)
        own_values = jax.vmap(lambda x, n: jnp.take(x, n, axis=0))(solved, coarse_number).reshape(N_GRP, N_SUB, NCL, RHS)
        fine = products(neumann_flat, weighted.reshape(flat)).reshape(whole)
        correction = fine + jnp.einsum("gsin,gsnk->gsik", basis_wide, own_values, precision=highest)
        scaled = weights * correction
        update = scaled + partner(scaled)
        current = (current.astype(jnp.float32) + update).astype(jnp.bfloat16)
    return current
```

```python
import jax
import jax.numpy as jnp
from jax import lax
from jax.experimental import pallas as pl
from jax.experimental.pallas import tpu as pltpu
from jax.sharding import PartitionSpec as P

ITERS = 3
FACE = 256
MESH = pl.DeviceIdType.MESH
FAR_FIRST = (4, 3, 5, 2, 6, 1, 7)
F32, BF16 = jnp.float32, jnp.bfloat16


def dot(a, b):
    return jnp.dot(a, b, preferred_element_type=F32)


def halves(x):
    high = x.astype(BF16)
    return high, (x - high.astype(F32)).astype(BF16)


def kernel(
    s_hbm, n_hbm, w_hbm, bt_hbm, inv_hbm, num_hbm, l_hbm, x_hbm, o_ref,
    s_ref, n_ref, w_ref, bt_ref, inv_ref, num_ref, l_ref, wb, bb, wt, u_keep, inv16, planes, turns, cols_ref, rows_ref,
    ex_src, ex_dst, up_src, up_dst, c_all, part, part_in, own_src, own_dst,
    ga_src, ga_dst, slab1, slab2, all1, all2, a_hi, a_lo, nb_src, nb_dst,
    load_sem, ex_s, ex_r, up_s, up_r, c1_s, c1_r, c2_s, c2_r, ow_s, ow_r, ga_s, ga_r, gb_s, gb_r, nb_s, nb_r,
):
    g, s = lax.axis_index("grp"), lax.axis_index("sub")
    z, yc = s // 8, s % 8
    near = [(g, (s + 63) % 64), (g, (s + 1) % 64), ((g + 7) % 8, s), ((g + 1) % 8, s)]
    mate = [1, 0, 3, 2]

    def z_peer(k):
        return (g, ((z + k) % 8) * 8 + yc)

    def yc_peer(k):
        return (g, z * 8 + (yc + k) % 8)

    def rc(src, dst, ssem, rsem, dev):
        return pltpu.make_async_remote_copy(
            src_ref=src, dst_ref=dst, send_sem=ssem, recv_sem=rsem, device_id=dev, device_id_type=MESH
        )

    def face(f):
        return pl.ds(f * FACE, FACE)

    def ex_copy(it, f):
        m = mate[f]
        return rc(ex_src.at[it, face(f)], ex_dst.at[it, face(m)], ex_s.at[it, f], ex_r.at[it, m], near[f])

    def up_copy(it, f):
        m = mate[f]
        return rc(up_src.at[it, face(f)], up_dst.at[it, face(m)], up_s.at[it, f], up_r.at[it, m], near[f])

    def ow_copy(it, f):
        m = mate[f]
        return rc(own_src.at[it], own_dst.at[it, m], ow_s.at[it, f], ow_r.at[it, m], near[f])

    def nb_copy(f):
        m = mate[f]
        return rc(nb_src.at[f], nb_dst.at[m], nb_s.at[f], nb_r.at[m], near[f])

    def c1_copy(it, k):
        mine = pl.ds(pl.multiple_of(z * 24, 8), 24)
        return rc(c_all.at[it, mine], c_all.at[it, mine], c1_s.at[it, k], c1_r.at[it, k], z_peer(k))

    def c2_copy(it, k):
        there = pl.ds(pl.multiple_of(((yc + k) % 8) * 24, 8), 24)
        return rc(part.at[it, there], part_in.at[it, k], c2_s.at[it, k], c2_r.at[it, k], yc_peer(k))

    def ga_copy(k):
        return rc(ga_src.at[(yc + k) % 8], ga_dst.at[yc], ga_s.at[k], ga_r.at[k], yc_peer(k))

    def gb_copy(k):
        here = pl.ds(pl.multiple_of(z * 96, 8), 96)
        return rc(slab1, all1.at[here], gb_s.at[0, k], gb_r.at[0, k], z_peer(k))

    def gc_copy(k):
        here = pl.ds(pl.multiple_of(z * 48, 8), 48)
        return rc(slab2, all2.at[here], gb_s.at[1, k], gb_r.at[1, k], z_peer(k))

    load_s, load_n, load_w, load_bt, load_inv, load_num, load_l, load_x = [
        pltpu.make_async_copy(a, b, load_sem.at[i])
        for i, (a, b) in enumerate(
            [(s_hbm, s_ref), (n_hbm, n_ref), (w_hbm, w_ref), (bt_hbm, bt_ref), (inv_hbm, inv_ref),
             (num_hbm, num_ref), (l_hbm, l_ref), (x_hbm, o_ref)]
        )
    ]
    for load in (load_num, load_inv, load_bt, load_w, load_x, load_s, load_l, load_n):
        load.start()
    c_all[...] = jnp.zeros_like(c_all)

    barrier = pltpu.get_barrier_semaphore()
    for dev in near + [z_peer(k) for k in range(1, 8)] + [yc_peer(k) for k in range(1, 8)]:
        pl.semaphore_signal(barrier, inc=1, device_id=dev, device_id_type=MESH)

    load_num.wait()
    for q in range(8):
        at = (192 * q) // 128 * 128
        row = num_ref[:, at : at + 256]
        planes[q : q + 1, :] = row if q % 2 == 0 else pltpu.roll(row, 192, axis=1)
    for q in range(8):
        turned = planes[...] if q == 0 else pltpu.roll(planes[...], 256 - 24 * q, axis=1)
        for p in range(8):
            turns[p, q : q + 1, :] = turned[p : p + 1, :]
    lane = lax.broadcasted_iota(jnp.int32, (8, 256), 1)
    cols = jnp.where(lane < 24, turns[0], -1)
    for p in range(1, 8):
        here = (lane >= 24 * p) & (lane < 24 * p + 24)
        cols = jnp.where(here, pltpu.roll(turns[p], 24 * p, axis=1), cols)
    cols_ref[...] = cols
    n = planes[pl.ds(z, 1), :]
    zn = (n * 683) >> 16
    dn = (n * 5462) >> 16
    i, dn = n - 12 * dn, dn - 8 * zn
    r = jnp.where(i < 8, dn * 8 + i, 56 + dn * 4 + i)
    rows_ref[0:1, :] = zn * 96 + r
    rows_ref[1:2, :] = jnp.where(r < 48, zn * 48 + r, -1)
    rows_ref[2:3, :] = jnp.where(r >= 48, zn * 48 + r - 48, -1)

    load_inv.wait()
    inv16[...] = jnp.zeros_like(inv16)
    for q in range(8):
        inv16[q : q + 1, :] = inv_ref[q]
    for q in range(8, 12):
        inv16[pl.ds(q + 4 * (yc % 2), 1), :] = inv_ref[q]
    inv_hi, inv_lo = halves(inv16[...])
    pieces = jnp.concatenate([inv_hi, inv_lo], axis=0)
    order = lax.broadcasted_iota(jnp.int32, (768, 256), 0)

    def pick(q, carry):
        hot = jnp.where(order == cols_ref[pl.ds(q, 1), :], 1.0, 0.0).astype(BF16)
        both = dot(pieces, hot)
        ga_src[q] = both[:16] + both[16:]
        return carry

    lax.fori_loop(0, 8, pick, 0)
    load_bt.wait()
    basis = bt_ref[...].astype(F32)
    for f in range(4):
        nb_src[f] = basis[:, f * FACE : (f + 1) * FACE]

    pl.semaphore_wait(barrier, 18)
    for k in FAR_FIRST:
        ga_copy(k).start()
    ga_dst[yc] = ga_src[yc]
    for f in range(4):
        nb_copy(f).start()

    load_w.wait()
    for q in range(8):
        wide = jnp.broadcast_to(w_ref[q : q + 1, :], (128, 128))
        wb[q * 128 : (q + 1) * 128, :] = wide.T

    load_x.wait()
    load_s.wait()
    load_l.wait()

    def send_part(it, current):
        for f in (1, 0, 3, 2):
            image = dot(s_ref[face(f), :], current)
            ex_src[it, face(f), :] = l_ref[face(f), :].astype(F32) - image
            ex_copy(it, f).start()

    def make_slabs():
        for k in range(1, 8):
            ga_copy(k).wait_recv()
        low = [ga_dst[q, 0:8, :] for q in range(8)]
        high = [ga_dst[2 * q, 8:16, :] + ga_dst[2 * q + 1, 8:16, :] for q in range(4)]
        slab = jnp.concatenate(low + high, axis=0)
        slab1[...] = slab[:, 0:128]
        slab2[...] = slab[0:48, 128:256] + pltpu.roll(slab[48:96, 128:256], 64, axis=1)
        for k in FAR_FIRST:
            gb_copy(k).start()
            gc_copy(k).start()
        all1[pl.ds(pl.multiple_of(z * 96, 8), 96), :] = slab1[...]
        all2[pl.ds(pl.multiple_of(z * 48, 8), 48), :] = slab2[...]

    def make_basis():
        for f in range(4):
            nb_copy(f).wait_recv()
        for f in range(4):
            own, other = nb_src[f], nb_dst[f]
            rows = jnp.concatenate([own, own, other, other, jnp.zeros((32, FACE), F32)], axis=0)
            for h in range(2):
                at = f * FACE + h * 128
                bb[at : at + 128, :] = rows[:, h * 128 : (h + 1) * 128].T.astype(BF16)

    def make_a():
        for k in range(1, 8):
            gb_copy(k).wait_recv()
            gc_copy(k).wait_recv()

        def column(at):
            return jnp.broadcast_to(rows_ref[at : at + 1, :], (128, 256)).T[0:192, :]

        def hot(at, width):
            wanted = column(at)
            lane = lax.broadcasted_iota(jnp.int32, (192, 128), 1)
            return jnp.concatenate(
                [jnp.where(wanted == lane + 128 * i, 1.0, 0.0).astype(BF16) for i in range(width // 128)], axis=1
            )

        first = dot(hot(0, 768), jnp.concatenate(halves(all1[...]), axis=1))
        two = jnp.concatenate(halves(all2[...]), axis=1)
        left, right = dot(hot(1, 384), two), dot(hot(2, 384), two)
        lane = lax.broadcasted_iota(jnp.int32, (192, 128), 1)
        for out, at in ((a_hi, 0), (a_lo, 128)):
            tail = left[:, at : at + 128] + 0.0
            other = pltpu.roll(right[:, at : at + 128], 64, axis=1)
            tail = jnp.where(lane < 64, tail, 0.0) + jnp.where(lane < 64, other, 0.0)
            out[...] = jnp.concatenate([first[:, at : at + 128], tail], axis=1).astype(BF16)

    def step(it, carry):
        @pl.when(it == 0)
        def _():
            make_slabs()

        mine = pl.ds(pl.multiple_of(z * 24, 8), 24)
        local = jnp.zeros((24, 128), F32)
        for f in (2, 3, 0, 1):
            ex_copy(it, mate[f]).wait_recv()
            resid = ex_src[it, face(f), :] + ex_dst[it, face(f), :]
            weighted = (wb[face(f), :] * resid).astype(BF16)
            wt[face(f), :] = weighted
            local = local + dot(bt_ref[:, f * FACE : (f + 1) * FACE], weighted)
        c_all[it, mine, :] = local
        for k in FAR_FIRST:
            c1_copy(it, k).start()

        @pl.when(it == 0)
        def _():
            load_n.wait()

        for f in (1, 0, 3, 2):
            up_src[it, face(f), :] = wb[face(f), :] * dot(n_ref[face(f), :], wt[...])
            up_copy(it, f).start()

        @pl.when(it == 0)
        def _():
            make_basis()
            make_a()

        for k in range(1, 8):
            c1_copy(it, k).wait_recv()
        high, low = halves(c_all[it])
        part[it] = dot(a_hi[...], high) + dot(a_hi[...], low) + dot(a_lo[...], high)
        for k in FAR_FIRST:
            c2_copy(it, k).start()
        total = part[it, pl.ds(pl.multiple_of(yc * 24, 8), 24), :]
        for k in range(1, 8):
            c2_copy(it, k).wait_recv()
            total = total + part_in[it, k]
        own_src[it] = total
        for f in (1, 0, 3, 2):
            ow_copy(it, f).start()
        for f in range(4):
            up_copy(it, mate[f]).wait_recv()
            u_keep[face(f), :] = x_now[face(f), :].astype(F32) + (up_src[it, face(f), :] + up_dst[it, face(f), :])
        own_hi = total.astype(BF16).astype(F32)
        zeros24, zeros80 = jnp.zeros((48, 128), F32), jnp.zeros((80, 128), F32)
        for f in (2, 3, 0, 1):
            ow_copy(it, mate[f]).wait_recv()
            other = own_dst[it, f]
            other_hi = other.astype(BF16).astype(F32)
            mine_in = jnp.concatenate([own_hi, total - own_hi, zeros80], axis=0).astype(BF16)
            other_in = jnp.concatenate([zeros24, other_hi, other - other_hi, zeros80[:32]], axis=0).astype(BF16)
            w = wb[face(f), :]
            coarse = w * dot(bb[face(f), :], mine_in) + (1.0 - w) * dot(bb[face(f), :], other_in)
            x_now[face(f), :] = (u_keep[face(f), :] + coarse).astype(BF16)

        @pl.when(it + 1 < ITERS)
        def _():
            send_part(it + 1, x_now[...])

        return carry

    x_now = o_ref
    send_part(0, x_now[...])
    lax.fori_loop(0, ITERS, step, 0)

    def drain(it, carry):
        for f in range(4):
            ex_copy(it, f).wait_send()
            up_copy(it, f).wait_send()
            ow_copy(it, f).wait_send()
        for k in range(1, 8):
            c1_copy(it, k).wait_send()
            c2_copy(it, k).wait_send()
        return carry

    lax.fori_loop(0, ITERS, drain, 0)
    for f in range(4):
        nb_copy(f).wait_send()
    for k in range(1, 8):
        ga_copy(k).wait_send()
        gb_copy(k).wait_send()
        gc_copy(k).wait_send()


def shards(schur_t, neumann_t, face_weights, coarse_basis, coarse_inverse, coarse_number, loads, iterate):
    weights = face_weights.reshape(8, 128)
    basis_t = coarse_basis[0, 0].T
    vmem = pl.BlockSpec(memory_space=pltpu.VMEM)
    hbm = pl.BlockSpec(memory_space=pl.ANY)
    dma = pltpu.SemaphoreType.DMA
    out = pl.pallas_call(
        kernel,
        name="bddc_steps",
        out_shape=jax.ShapeDtypeStruct((1024, 128), BF16),
        in_specs=[hbm] * 8,
        out_specs=vmem,
        scratch_shapes=[
            pltpu.VMEM((1024, 1024), BF16),
            pltpu.VMEM((1024, 1024), BF16),
            pltpu.VMEM((8, 128), F32),
            pltpu.VMEM((24, 1024), BF16),
            pltpu.VMEM((12, 1, 768), F32),
            pltpu.VMEM((1, 1536), jnp.int32),
            pltpu.VMEM((1024, 128), BF16),
            pltpu.VMEM((1024, 128), F32),
            pltpu.VMEM((1024, 128), BF16),
            pltpu.VMEM((1024, 128), BF16),
            pltpu.VMEM((1024, 128), F32),
            pltpu.VMEM((16, 768), F32),
            pltpu.VMEM((8, 256), jnp.int32),
            pltpu.VMEM((8, 8, 256), jnp.int32),
            pltpu.VMEM((8, 256), jnp.int32),
            pltpu.VMEM((8, 256), jnp.int32),
            pltpu.VMEM((ITERS, 1024, 128), F32),
            pltpu.VMEM((ITERS, 1024, 128), F32),
            pltpu.VMEM((ITERS, 1024, 128), F32),
            pltpu.VMEM((ITERS, 1024, 128), F32),
            pltpu.VMEM((ITERS, 256, 128), F32),
            pltpu.VMEM((ITERS, 192, 128), F32),
            pltpu.VMEM((ITERS, 8, 24, 128), F32),
            pltpu.VMEM((ITERS, 24, 128), F32),
            pltpu.VMEM((ITERS, 4, 24, 128), F32),
            pltpu.VMEM((8, 16, 256), F32),
            pltpu.VMEM((8, 16, 256), F32),
            pltpu.VMEM((96, 128), F32),
            pltpu.VMEM((48, 128), F32),
            pltpu.VMEM((768, 128), F32),
            pltpu.VMEM((384, 128), F32),
            pltpu.VMEM((192, 256), BF16),
            pltpu.VMEM((192, 256), BF16),
            pltpu.VMEM((4, 24, 256), F32),
            pltpu.VMEM((4, 24, 256), F32),
            dma((8,)),
            dma((ITERS, 4)), dma((ITERS, 4)),
            dma((ITERS, 4)), dma((ITERS, 4)),
            dma((ITERS, 8)), dma((ITERS, 8)),
            dma((ITERS, 8)), dma((ITERS, 8)),
            dma((ITERS, 4)), dma((ITERS, 4)),
            dma((8,)), dma((8,)),
            dma((2, 8)), dma((2, 8)),
            dma((4,)), dma((4,)),
        ],
        compiler_params=pltpu.CompilerParams(
            collective_id=0, has_side_effects=True, vmem_limit_bytes=67000000
        ),
    )(schur_t[0, 0], neumann_t[0, 0], weights, basis_t, coarse_inverse.reshape(12, 1, 768), coarse_number, loads[0, 0], iterate[0, 0])
    return out[None, None]


def solution(mesh):
    return jax.shard_map(
        shards,
        mesh=mesh,
        in_specs=(
            P("grp", "sub", None, None),
            P("grp", "sub", None, None),
            P("grp", "sub", None),
            P("grp", "sub", None, None),
            P("grp", "sub", None),
            P("grp", None),
            P("grp", "sub", None, None),
            P("grp", "sub", None, None),
        ),
        out_specs=P("grp", "sub", None, None),
        check_vma=False,
    )
```

```python
import jax
import jax.numpy as jnp
from jax import lax
from jax.experimental import pallas as pl
from jax.experimental.pallas import tpu as pltpu
from jax.sharding import PartitionSpec as P

ITERS = 3
FACE = 256
MESH = pl.DeviceIdType.MESH
FAR_FIRST = (4, 3, 5, 2, 6, 1, 7)
AROUND = (
    (0, 0), (0, -1), (0, 1), (-1, 0), (1, 0),
    (0, -2), (0, 2), (-2, 0), (2, 0), (-1, -1), (-1, 1), (1, -1), (1, 1),
)


def place(*steps):
    return AROUND.index((sum(a for a, _ in steps), sum(b for _, b in steps)))


FIVE = [[place(AROUND[i], AROUND[j]) for j in range(5)] for i in range(5)]
BACK = [AROUND.index((-a, -b)) for a, b in AROUND]
F32, BF16 = jnp.float32, jnp.bfloat16


def dot(a, b):
    return jnp.dot(a, b, preferred_element_type=F32)


def halves(x):
    high = x.astype(BF16)
    return high, (x - high.astype(F32)).astype(BF16)


def kernel(
    s_hbm, n_hbm, w_hbm, bt_hbm, inv_hbm, num_hbm, l_hbm, x_hbm, o_ref,
    s_ref, n_ref, w_ref, bt_ref, inv_ref, num_ref, l_ref, wb, b5, wt, x_fine, corr, t_src, t_dst, t_hi, t_lo, inv16, planes, turns, cols_ref, rows_ref,
    ex_src, ex_dst, up_src, up_dst, c_all, part, part_in, own,
    ga_src, ga_dst, slab1, slab2, all1, all2, a_hi, a_lo, nb_src, nb_dst,
    load_sem, ex_s, ex_r, up_s, up_r, c1_s, c1_r, c2_s, c2_r, ow_s, ow_r, ga_s, ga_r, gb_s, gb_r, nb_s, nb_r, t_s, t_r,
):
    g, s = lax.axis_index("grp"), lax.axis_index("sub")
    z, yc = s // 8, s % 8
    near = [(g, (s + 63) % 64), (g, (s + 1) % 64), ((g + 7) % 8, s), ((g + 1) % 8, s)]
    mate = [1, 0, 3, 2]
    around = [((g + (8 + dg)) % 8, (s + (64 + ds)) % 64) for dg, ds in AROUND[1:]]

    def z_peer(k):
        return (g, ((z + k) % 8) * 8 + yc)

    def yc_peer(k):
        return (g, z * 8 + (yc + k) % 8)

    def rc(src, dst, ssem, rsem, dev):
        return pltpu.make_async_remote_copy(
            src_ref=src, dst_ref=dst, send_sem=ssem, recv_sem=rsem, device_id=dev, device_id_type=MESH
        )

    def face(f):
        return pl.ds(f * FACE, FACE)

    def ex_copy(it, f):
        m = mate[f]
        return rc(ex_src.at[it, face(f)], ex_dst.at[it, face(m)], ex_s.at[it, f], ex_r.at[it, m], near[f])

    def up_copy(it, f):
        m = mate[f]
        return rc(up_src.at[it, face(f)], up_dst.at[it, face(m)], up_s.at[it, f], up_r.at[it, m], near[f])

    def ow_copy(it, i):
        dg, ds = AROUND[i]
        there = ((g + (8 + dg)) % 8, (s + (64 + ds)) % 64)
        return rc(own.at[it, 0], own.at[it, BACK[i]], ow_s.at[it, i], ow_r.at[it, BACK[i]], there)

    def t_copy(f):
        m = mate[f]
        return rc(t_src.at[face(f)], t_dst.at[face(m)], t_s.at[f], t_r.at[m], near[f])

    def nb_copy(f):
        m = mate[f]
        return rc(nb_src.at[f], nb_dst.at[m], nb_s.at[f], nb_r.at[m], near[f])

    def c1_copy(it, k):
        mine = pl.ds(pl.multiple_of(z * 24, 8), 24)
        return rc(c_all.at[it, mine], c_all.at[it, mine], c1_s.at[it, k], c1_r.at[it, k], z_peer(k))

    def c2_copy(it, k):
        there = pl.ds(pl.multiple_of(((yc + k) % 8) * 24, 8), 24)
        return rc(part.at[it, there], part_in.at[it, k], c2_s.at[it, k], c2_r.at[it, k], yc_peer(k))

    def ga_copy(k):
        return rc(ga_src.at[(yc + k) % 8], ga_dst.at[yc], ga_s.at[k], ga_r.at[k], yc_peer(k))

    def gb_copy(k):
        here = pl.ds(pl.multiple_of(z * 96, 8), 96)
        return rc(slab1, all1.at[here], gb_s.at[0, k], gb_r.at[0, k], z_peer(k))

    def gc_copy(k):
        here = pl.ds(pl.multiple_of(z * 48, 8), 48)
        return rc(slab2, all2.at[here], gb_s.at[1, k], gb_r.at[1, k], z_peer(k))

    load_s, load_n, load_w, load_bt, load_inv, load_num, load_l, load_x = [
        pltpu.make_async_copy(a, b, load_sem.at[i])
        for i, (a, b) in enumerate(
            [(s_hbm, s_ref), (n_hbm, n_ref), (w_hbm, w_ref), (bt_hbm, bt_ref), (inv_hbm, inv_ref),
             (num_hbm, num_ref), (l_hbm, l_ref), (x_hbm, o_ref)]
        )
    ]
    for load in (load_num, load_inv, load_bt, load_w, load_x, load_s, load_l, load_n):
        load.start()
    c_all[...] = jnp.zeros_like(c_all)
    corr[...] = jnp.zeros_like(corr)

    barrier = pltpu.get_barrier_semaphore()
    for dev in around + [z_peer(k) for k in range(1, 8)] + [yc_peer(k) for k in range(1, 8)]:
        pl.semaphore_signal(barrier, inc=1, device_id=dev, device_id_type=MESH)

    load_num.wait()
    for q in range(8):
        at = (192 * q) // 128 * 128
        row = num_ref[:, at : at + 256]
        planes[q : q + 1, :] = row if q % 2 == 0 else pltpu.roll(row, 192, axis=1)
    for q in range(8):
        turned = planes[...] if q == 0 else pltpu.roll(planes[...], 256 - 24 * q, axis=1)
        for p in range(8):
            turns[p, q : q + 1, :] = turned[p : p + 1, :]
    lane = lax.broadcasted_iota(jnp.int32, (8, 256), 1)
    cols = jnp.where(lane < 24, turns[0], -1)
    for p in range(1, 8):
        here = (lane >= 24 * p) & (lane < 24 * p + 24)
        cols = jnp.where(here, pltpu.roll(turns[p], 24 * p, axis=1), cols)
    cols_ref[...] = cols
    n = planes[pl.ds(z, 1), :]
    zn = (n * 683) >> 16
    dn = (n * 5462) >> 16
    i, dn = n - 12 * dn, dn - 8 * zn
    r = jnp.where(i < 8, dn * 8 + i, 56 + dn * 4 + i)
    rows_ref[0:1, :] = zn * 96 + r
    rows_ref[1:2, :] = jnp.where(r < 48, zn * 48 + r, -1)
    rows_ref[2:3, :] = jnp.where(r >= 48, zn * 48 + r - 48, -1)

    load_inv.wait()
    inv16[...] = jnp.zeros_like(inv16)
    for q in range(8):
        inv16[q : q + 1, :] = inv_ref[q]
    for q in range(8, 12):
        inv16[pl.ds(q + 4 * (yc % 2), 1), :] = inv_ref[q]
    inv_hi, inv_lo = halves(inv16[...])
    pieces = jnp.concatenate([inv_hi, inv_lo], axis=0)
    order = lax.broadcasted_iota(jnp.int32, (768, 256), 0)

    def pick(q, carry):
        hot = jnp.where(order == cols_ref[pl.ds(q, 1), :], 1.0, 0.0).astype(BF16)
        both = dot(pieces, hot)
        ga_src[q] = both[:16] + both[16:]
        return carry

    lax.fori_loop(0, 8, pick, 0)
    load_bt.wait()
    basis = bt_ref[...].astype(F32)
    for f in range(4):
        nb_src[f] = basis[:, f * FACE : (f + 1) * FACE]

    pl.semaphore_wait(barrier, 26)
    for k in FAR_FIRST:
        ga_copy(k).start()
    ga_dst[yc] = ga_src[yc]
    for f in range(4):
        nb_copy(f).start()

    load_w.wait()
    for q in range(8):
        wide = jnp.broadcast_to(w_ref[q : q + 1, :], (128, 128))
        wb[q * 128 : (q + 1) * 128, :] = wide.T

    load_x.wait()
    load_s.wait()
    load_l.wait()

    def send_part(it, current):
        for f in (1, 0, 3, 2):
            image = dot(s_ref[face(f), :], current)
            ex_src[it, face(f), :] = l_ref[face(f), :].astype(F32) - image
            ex_copy(it, f).start()

    def make_slabs():
        for k in range(1, 8):
            ga_copy(k).wait_recv()
        low = [ga_dst[q, 0:8, :] for q in range(8)]
        high = [ga_dst[2 * q, 8:16, :] + ga_dst[2 * q + 1, 8:16, :] for q in range(4)]
        slab = jnp.concatenate(low + high, axis=0)
        slab1[...] = slab[:, 0:128]
        slab2[...] = slab[0:48, 128:256] + pltpu.roll(slab[48:96, 128:256], 64, axis=1)
        for k in FAR_FIRST:
            gb_copy(k).start()
            gc_copy(k).start()
        all1[pl.ds(pl.multiple_of(z * 96, 8), 96), :] = slab1[...]
        all2[pl.ds(pl.multiple_of(z * 48, 8), 48), :] = slab2[...]

    def make_basis():
        for f in range(4):
            nb_copy(f).wait_recv()
        lane = lax.broadcasted_iota(jnp.int32, (128, 128), 1)
        none = jnp.zeros((24, FACE), F32)
        for f in range(4):
            rows = [nb_src[f]] + [nb_dst[f] if j == f else none for j in range(4)] + [none[:8]]
            rows = jnp.concatenate(rows, axis=0)
            for h in range(2):
                at = f * FACE + h * 128
                w = wb[at : at + 128, :]
                scaled = jnp.where(lane < 24, w, 1.0 - w) * rows[:, h * 128 : (h + 1) * 128].T
                b5[at : at + 128, :] = jnp.concatenate(halves(scaled), axis=1)
        for f in (1, 0, 3, 2):
            both = dot(s_ref[face(f), :], b5[...])
            t_src[face(f), :] = both[:, :128] + both[:, 128:]
            t_copy(f).start()

    def make_t():
        for f in range(4):
            t_copy(mate[f]).wait_recv()
            (mine_hi, mine_lo), (other_hi, other_lo) = halves(t_src[face(f), :]), halves(t_dst[face(f), :])
            t_hi[face(f), :] = jnp.concatenate([mine_hi, other_hi], axis=1)
            t_lo[face(f), :] = jnp.concatenate([mine_lo, other_lo], axis=1)

    def five(it, i):
        return [own[it, j] for j in FIVE[i]] + [jnp.zeros((8, 128), F32)]

    def finish(it):
        high, low = halves(jnp.concatenate(five(it, 0), axis=0))
        pair = jnp.concatenate([high, low], axis=1)
        for f in range(4):
            both = dot(b5[face(f), 0:128], pair)
            coarse = both[:, :128] + both[:, 128:] + dot(b5[face(f), 128:256], high)
            x_now[face(f), :] = (x_fine[face(f), :] + coarse).astype(BF16)

    def make_a():
        for k in range(1, 8):
            gb_copy(k).wait_recv()
            gc_copy(k).wait_recv()

        def column(at):
            return jnp.broadcast_to(rows_ref[at : at + 1, :], (128, 256)).T[0:192, :]

        def hot(at, width):
            wanted = column(at)
            lane = lax.broadcasted_iota(jnp.int32, (192, 128), 1)
            return jnp.concatenate(
                [jnp.where(wanted == lane + 128 * i, 1.0, 0.0).astype(BF16) for i in range(width // 128)], axis=1
            )

        first = dot(hot(0, 768), jnp.concatenate(halves(all1[...]), axis=1))
        two = jnp.concatenate(halves(all2[...]), axis=1)
        left, right = dot(hot(1, 384), two), dot(hot(2, 384), two)
        lane = lax.broadcasted_iota(jnp.int32, (192, 128), 1)
        for out, at in ((a_hi, 0), (a_lo, 128)):
            tail = left[:, at : at + 128] + 0.0
            other = pltpu.roll(right[:, at : at + 128], 64, axis=1)
            tail = jnp.where(lane < 64, tail, 0.0) + jnp.where(lane < 64, other, 0.0)
            out[...] = jnp.concatenate([first[:, at : at + 128], tail], axis=1).astype(BF16)

    def step(it, carry):
        @pl.when(it == 0)
        def _():
            make_slabs()

        mine = pl.ds(pl.multiple_of(z * 24, 8), 24)
        local = jnp.zeros((24, 128), F32)
        for f in (2, 3, 0, 1):
            ex_copy(it, mate[f]).wait_recv()
            resid = ex_src[it, face(f), :] + ex_dst[it, face(f), :] - corr[face(f), :]
            weighted = (wb[face(f), :] * resid).astype(BF16)
            wt[face(f), :] = weighted
            local = local + dot(bt_ref[:, f * FACE : (f + 1) * FACE], weighted)
        c_all[it, mine, :] = local
        for k in FAR_FIRST:
            c1_copy(it, k).start()

        @pl.when(it == 0)
        def _():
            load_n.wait()

        for f in (1, 0, 3, 2):
            up_src[it, face(f), :] = wb[face(f), :] * dot(n_ref[face(f), :], wt[...])
            up_copy(it, f).start()

        @pl.when(it == 0)
        def _():
            make_basis()
            make_a()

        @pl.when(it > 0)
        def _():
            finish(it - 1)

        for k in range(1, 8):
            c1_copy(it, k).wait_recv()
        high, low = halves(c_all[it])
        part[it] = dot(a_hi[...], high) + dot(a_hi[...], low) + dot(a_lo[...], high)
        for k in FAR_FIRST:
            c2_copy(it, k).start()
        for f in range(4):
            up_copy(it, mate[f]).wait_recv()
            x_fine[face(f), :] = x_now[face(f), :].astype(F32) + (up_src[it, face(f), :] + up_dst[it, face(f), :])

        @pl.when(it + 1 < ITERS)
        def _():
            send_part(it + 1, x_fine[...].astype(BF16))

        total = part[it, pl.ds(pl.multiple_of(yc * 24, 8), 24), :]
        for k in range(1, 8):
            c2_copy(it, k).wait_recv()
            total = total + part_in[it, k]
        own[it, 0] = total
        for i in (2, 1, 4, 3):
            ow_copy(it, i).start()

        @pl.when(it + 1 < ITERS)
        def _():
            for i in (9, 10, 11, 12, 5, 6, 7, 8):
                ow_copy(it, i).start()

            @pl.when(it == 0)
            def _():
                make_t()

            for i in range(1, 13):
                ow_copy(it, i).wait_recv()
            here = five(it, 0)
            for f in range(4):
                high, low = halves(jnp.concatenate(here + five(it, 1 + f), axis=0))
                both = dot(t_hi[face(f), :], jnp.concatenate([high, low], axis=1))
                corr[face(f), :] = both[:, :128] + both[:, 128:] + dot(t_lo[face(f), :], high)

        return carry

    x_now = o_ref
    send_part(0, x_now[...])
    lax.fori_loop(0, ITERS, step, 0)
    for i in range(1, 5):
        ow_copy(ITERS - 1, i).wait_recv()
    finish(ITERS - 1)

    def drain(it, carry):
        for f in range(4):
            ex_copy(it, f).wait_send()
            up_copy(it, f).wait_send()
            ow_copy(it, f + 1).wait_send()
        for k in range(1, 8):
            c1_copy(it, k).wait_send()
            c2_copy(it, k).wait_send()

        @pl.when(it + 1 < ITERS)
        def _():
            for i in range(5, 13):
                ow_copy(it, i).wait_send()

        return carry

    lax.fori_loop(0, ITERS, drain, 0)
    for f in range(4):
        nb_copy(f).wait_send()
        t_copy(f).wait_send()
    for k in range(1, 8):
        ga_copy(k).wait_send()
        gb_copy(k).wait_send()
        gc_copy(k).wait_send()


def shards(schur_t, neumann_t, face_weights, coarse_basis, coarse_inverse, coarse_number, loads, iterate):
    weights = face_weights.reshape(8, 128)
    basis_t = coarse_basis[0, 0].T
    vmem = pl.BlockSpec(memory_space=pltpu.VMEM)
    hbm = pl.BlockSpec(memory_space=pl.ANY)
    dma = pltpu.SemaphoreType.DMA
    out = pl.pallas_call(
        kernel,
        name="bddc_steps",
        out_shape=jax.ShapeDtypeStruct((1024, 128), BF16),
        in_specs=[hbm] * 8,
        out_specs=vmem,
        scratch_shapes=[
            pltpu.VMEM((1024, 1024), BF16),
            pltpu.VMEM((1024, 1024), BF16),
            pltpu.VMEM((8, 128), F32),
            pltpu.VMEM((24, 1024), BF16),
            pltpu.VMEM((12, 1, 768), F32),
            pltpu.VMEM((1, 1536), jnp.int32),
            pltpu.VMEM((1024, 128), BF16),
            pltpu.VMEM((1024, 128), F32),
            pltpu.VMEM((1024, 256), BF16),
            pltpu.VMEM((1024, 128), BF16),
            pltpu.VMEM((1024, 128), F32),
            pltpu.VMEM((1024, 128), F32),
            pltpu.VMEM((1024, 128), F32),
            pltpu.VMEM((1024, 128), F32),
            pltpu.VMEM((1024, 256), BF16),
            pltpu.VMEM((1024, 256), BF16),
            pltpu.VMEM((16, 768), F32),
            pltpu.VMEM((8, 256), jnp.int32),
            pltpu.VMEM((8, 8, 256), jnp.int32),
            pltpu.VMEM((8, 256), jnp.int32),
            pltpu.VMEM((8, 256), jnp.int32),
            pltpu.VMEM((ITERS, 1024, 128), F32),
            pltpu.VMEM((ITERS, 1024, 128), F32),
            pltpu.VMEM((ITERS, 1024, 128), F32),
            pltpu.VMEM((ITERS, 1024, 128), F32),
            pltpu.VMEM((ITERS, 256, 128), F32),
            pltpu.VMEM((ITERS, 192, 128), F32),
            pltpu.VMEM((ITERS, 8, 24, 128), F32),
            pltpu.VMEM((ITERS, 13, 24, 128), F32),
            pltpu.VMEM((8, 16, 256), F32),
            pltpu.VMEM((8, 16, 256), F32),
            pltpu.VMEM((96, 128), F32),
            pltpu.VMEM((48, 128), F32),
            pltpu.VMEM((768, 128), F32),
            pltpu.VMEM((384, 128), F32),
            pltpu.VMEM((192, 256), BF16),
            pltpu.VMEM((192, 256), BF16),
            pltpu.VMEM((4, 24, 256), F32),
            pltpu.VMEM((4, 24, 256), F32),
            dma((8,)),
            dma((ITERS, 4)), dma((ITERS, 4)),
            dma((ITERS, 4)), dma((ITERS, 4)),
            dma((ITERS, 8)), dma((ITERS, 8)),
            dma((ITERS, 8)), dma((ITERS, 8)),
            dma((ITERS, 13)), dma((ITERS, 13)),
            dma((8,)), dma((8,)),
            dma((2, 8)), dma((2, 8)),
            dma((4,)), dma((4,)),
            dma((4,)), dma((4,)),
        ],
        compiler_params=pltpu.CompilerParams(
            collective_id=0, has_side_effects=True, vmem_limit_bytes=67000000
        ),
    )(schur_t[0, 0], neumann_t[0, 0], weights, basis_t, coarse_inverse.reshape(12, 1, 768), coarse_number, loads[0, 0], iterate[0, 0])
    return out[None, None]


def solution(mesh):
    return jax.shard_map(
        shards,
        mesh=mesh,
        in_specs=(
            P("grp", "sub", None, None),
            P("grp", "sub", None, None),
            P("grp", "sub", None),
            P("grp", "sub", None, None),
            P("grp", "sub", None),
            P("grp", None),
            P("grp", "sub", None, None),
            P("grp", "sub", None, None),
        ),
        out_specs=P("grp", "sub", None, None),
        check_vma=False,
    )
```

```python
import jax
import jax.numpy as jnp
from jax import lax
from jax.experimental import pallas as pl
from jax.experimental.pallas import tpu as pltpu
from jax.sharding import PartitionSpec as P

ITERS = 3
FACE = 256
MESH = pl.DeviceIdType.MESH
FAR_FIRST = (4, 3, 5, 2, 6, 1, 7)
AROUND = (
    (0, 0), (0, -1), (0, 1), (-1, 0), (1, 0),
    (0, -2), (0, 2), (-2, 0), (2, 0), (-1, -1), (-1, 1), (1, -1), (1, 1),
)


def place(*steps):
    return AROUND.index((sum(a for a, _ in steps), sum(b for _, b in steps)))


FIVE = [[place(AROUND[i], AROUND[j]) for j in range(5)] for i in range(5)]
BACK = [AROUND.index((-a, -b)) for a, b in AROUND]
F32, BF16 = jnp.float32, jnp.bfloat16


def dot(a, b):
    return jnp.dot(a, b, preferred_element_type=F32)


def halves(x):
    high = x.astype(BF16)
    return high, (x - high.astype(F32)).astype(BF16)


def kernel(
    s_hbm, n_hbm, w_hbm, bt_hbm, inv_hbm, num_hbm, l_hbm, x_hbm, o_ref,
    s_ref, n_ref, w_ref, bt_ref, inv_ref, num_ref, l_ref, wb, b5, wt, x_fine, corr, t_src, t_dst, t_hi, t_lo, inv16, planes, turns, cols_ref, rows_ref,
    ex_src, ex_dst, up_src, up_dst, c_all, part, part_in, own,
    ga_src, ga_dst, slab1, slab2, all1, all2, a_hi, a_lo, nb_src, nb_dst,
    load_sem, ex_s, ex_r, up_s, up_r, c1_s, c1_r, c2_s, c2_r, ow_s, ow_r, ga_s, ga_r, gb_s, gb_r, nb_s, nb_r, t_s, t_r,
):
    g, s = lax.axis_index("grp"), lax.axis_index("sub")
    z, yc = s // 8, s % 8
    near = [(g, (s + 63) % 64), (g, (s + 1) % 64), ((g + 7) % 8, s), ((g + 1) % 8, s)]
    mate = [1, 0, 3, 2]
    around = [((g + (8 + dg)) % 8, (s + (64 + ds)) % 64) for dg, ds in AROUND[1:]]

    def z_peer(k):
        return (g, ((z + k) % 8) * 8 + yc)

    def yc_peer(k):
        return (g, z * 8 + (yc + k) % 8)

    def rc(src, dst, ssem, rsem, dev):
        return pltpu.make_async_remote_copy(
            src_ref=src, dst_ref=dst, send_sem=ssem, recv_sem=rsem, device_id=dev, device_id_type=MESH
        )

    def face(f):
        return pl.ds(f * FACE, FACE)

    def ex_copy(it, f):
        m = mate[f]
        return rc(ex_src.at[it, face(f)], ex_dst.at[it, face(m)], ex_s.at[it, f], ex_r.at[it, m], near[f])

    def up_copy(it, f):
        m = mate[f]
        return rc(up_src.at[it, face(f)], up_dst.at[it, face(m)], up_s.at[it, f], up_r.at[it, m], near[f])

    def ow_copy(it, i):
        dg, ds = AROUND[i]
        there = ((g + (8 + dg)) % 8, (s + (64 + ds)) % 64)
        return rc(own.at[it, 0], own.at[it, BACK[i]], ow_s.at[it, i], ow_r.at[it, BACK[i]], there)

    def t_copy(f):
        m = mate[f]
        return rc(t_src.at[face(f)], t_dst.at[face(m)], t_s.at[f], t_r.at[m], near[f])

    def nb_copy(f):
        m = mate[f]
        return rc(nb_src.at[f], nb_dst.at[m], nb_s.at[f], nb_r.at[m], near[f])

    def c1_copy(it, k):
        mine = pl.ds(pl.multiple_of(z * 24, 8), 24)
        return rc(c_all.at[it, mine], c_all.at[it, mine], c1_s.at[it, k], c1_r.at[it, k], z_peer(k))

    def c2_copy(it, k):
        there = pl.ds(pl.multiple_of(((yc + k) % 8) * 24, 8), 24)
        return rc(part.at[it, there], part_in.at[it, k], c2_s.at[it, k], c2_r.at[it, k], yc_peer(k))

    def ga_copy(k):
        return rc(ga_src.at[(yc + k) % 8], ga_dst.at[yc], ga_s.at[k], ga_r.at[k], yc_peer(k))

    def slab_at(p, rows):
        return pl.ds(pl.multiple_of(p * rows, 8), rows)

    def gb_copies(i):
        step = (2, 6, 1, 7, 1, 7)[i]
        owner = (z + (0, 0, 0, 0, 6, 2)[i]) % 8
        there = z_peer(step)
        src1, src2 = (slab1, slab2) if i < 4 else (all1.at[slab_at(owner, 96)], all2.at[slab_at(owner, 48)])
        return [
            rc(src1, all1.at[slab_at(owner, 96)], gb_s.at[0, i], gb_r.at[0, i], there),
            rc(src2, all2.at[slab_at(owner, 48)], gb_s.at[1, i], gb_r.at[1, i], there),
        ]

    def gc_copy(i):
        every, rows = ((all1, 96), (all2, 48))[i]
        here = slab_at((z + (6, 2)[i]) % 8, rows)
        return rc(every.at[here], every.at[here], gb_s.at[i, 6], gb_r.at[i, 6], z_peer((2, 6)[i]))

    load_s, load_n, load_w, load_bt, load_inv, load_num, load_l, load_x = [
        pltpu.make_async_copy(a, b, load_sem.at[i])
        for i, (a, b) in enumerate(
            [(s_hbm, s_ref), (n_hbm, n_ref), (w_hbm, w_ref), (bt_hbm, bt_ref), (inv_hbm, inv_ref),
             (num_hbm, num_ref), (l_hbm, l_ref), (x_hbm, o_ref)]
        )
    ]
    for load in (load_num, load_inv, load_bt, load_w, load_x, load_s, load_l, load_n):
        load.start()
    c_all[...] = jnp.zeros_like(c_all)
    corr[...] = jnp.zeros_like(corr)

    barrier = pltpu.get_barrier_semaphore()
    for dev in around + [z_peer(k) for k in range(1, 8)] + [yc_peer(k) for k in range(1, 8)]:
        pl.semaphore_signal(barrier, inc=1, device_id=dev, device_id_type=MESH)

    load_num.wait()
    for q in range(8):
        at = (192 * q) // 128 * 128
        row = num_ref[:, at : at + 256]
        planes[q : q + 1, :] = row if q % 2 == 0 else pltpu.roll(row, 192, axis=1)
    for q in range(8):
        turned = planes[...] if q == 0 else pltpu.roll(planes[...], 256 - 24 * q, axis=1)
        for p in range(8):
            turns[p, q : q + 1, :] = turned[p : p + 1, :]
    lane = lax.broadcasted_iota(jnp.int32, (8, 256), 1)
    cols = jnp.where(lane < 24, turns[0], -1)
    for p in range(1, 8):
        here = (lane >= 24 * p) & (lane < 24 * p + 24)
        cols = jnp.where(here, pltpu.roll(turns[p], 24 * p, axis=1), cols)
    cols_ref[...] = cols
    n = planes[pl.ds(z, 1), :]
    zn = (n * 683) >> 16
    dn = (n * 5462) >> 16
    i, dn = n - 12 * dn, dn - 8 * zn
    r = jnp.where(i < 8, dn * 8 + i, 56 + dn * 4 + i)
    rows_ref[0:1, :] = zn * 96 + r
    rows_ref[1:2, :] = jnp.where(r < 48, zn * 48 + r, -1)
    rows_ref[2:3, :] = jnp.where(r >= 48, zn * 48 + r - 48, -1)

    load_inv.wait()
    inv16[...] = jnp.zeros_like(inv16)
    for q in range(8):
        inv16[q : q + 1, :] = inv_ref[q]
    for q in range(8, 12):
        inv16[pl.ds(q + 4 * (yc % 2), 1), :] = inv_ref[q]
    inv_hi, inv_lo = halves(inv16[...])
    pieces = jnp.concatenate([inv_hi, inv_lo], axis=0)
    order = lax.broadcasted_iota(jnp.int32, (768, 256), 0)

    def pick(q, carry):
        hot = jnp.where(order == cols_ref[pl.ds(q, 1), :], 1.0, 0.0).astype(BF16)
        both = dot(pieces, hot)
        ga_src[q] = both[:16] + both[16:]
        return carry

    lax.fori_loop(0, 8, pick, 0)
    load_bt.wait()
    basis = bt_ref[...].astype(F32)
    for f in range(4):
        nb_src[f] = basis[:, f * FACE : (f + 1) * FACE]

    ga_dst[yc] = ga_src[yc]
    load_w.wait()
    for q in range(8):
        wide = jnp.broadcast_to(w_ref[q : q + 1, :], (128, 128))
        wb[q * 128 : (q + 1) * 128, :] = wide.T

    load_x.wait()
    load_s.wait()
    load_l.wait()

    def make_part(it, current):
        for f in range(4):
            image = dot(s_ref[face(f), :], current)
            ex_src[it, face(f), :] = l_ref[face(f), :].astype(F32) - image

    def make_slabs():
        for k in range(1, 8):
            ga_copy(k).wait_recv()
        low = [ga_dst[q, 0:8, :] for q in range(8)]
        high = [ga_dst[2 * q, 8:16, :] + ga_dst[2 * q + 1, 8:16, :] for q in range(4)]
        slab = jnp.concatenate(low + high, axis=0)
        slab1[...] = slab[:, 0:128]
        slab2[...] = slab[0:48, 128:256] + pltpu.roll(slab[48:96, 128:256], 64, axis=1)
        for i in range(4):
            for copy in gb_copies(i):
                copy.start()
        all1[pl.ds(pl.multiple_of(z * 96, 8), 96), :] = slab1[...]
        all2[pl.ds(pl.multiple_of(z * 48, 8), 48), :] = slab2[...]

    def relay_slabs():
        for i in range(2):
            for copy in gb_copies(i):
                copy.wait_recv()
            for copy in gb_copies(4 + i):
                copy.start()
            gc_copy(i).start()

    def make_basis():
        for f in range(4):
            nb_copy(f).wait_recv()
        lane = lax.broadcasted_iota(jnp.int32, (128, 128), 1)
        none = jnp.zeros((24, FACE), F32)
        for f in range(4):
            rows = [nb_src[f]] + [nb_dst[f] if j == f else none for j in range(4)] + [none[:8]]
            rows = jnp.concatenate(rows, axis=0)
            for h in range(2):
                at = f * FACE + h * 128
                w = wb[at : at + 128, :]
                scaled = jnp.where(lane < 24, w, 1.0 - w) * rows[:, h * 128 : (h + 1) * 128].T
                b5[at : at + 128, :] = jnp.concatenate(halves(scaled), axis=1)
        for f in (1, 0, 3, 2):
            both = dot(s_ref[face(f), :], b5[...])
            t_src[face(f), :] = both[:, :128] + both[:, 128:]
            t_copy(f).start()

    def make_t():
        for f in range(4):
            t_copy(mate[f]).wait_recv()
            (mine_hi, mine_lo), (other_hi, other_lo) = halves(t_src[face(f), :]), halves(t_dst[face(f), :])
            t_hi[face(f), :] = jnp.concatenate([mine_hi, other_hi], axis=1)
            t_lo[face(f), :] = jnp.concatenate([mine_lo, other_lo], axis=1)

    def five(it, i):
        return [own[it, j] for j in FIVE[i]] + [jnp.zeros((8, 128), F32)]

    def finish(it):
        high, low = halves(jnp.concatenate(five(it, 0), axis=0))
        pair = jnp.concatenate([high, low], axis=1)
        for f in range(4):
            both = dot(b5[face(f), 0:128], pair)
            coarse = both[:, :128] + both[:, 128:] + dot(b5[face(f), 128:256], high)
            x_now[face(f), :] = (x_fine[face(f), :] + coarse).astype(BF16)

    def make_a():
        for i in range(2, 6):
            for copy in gb_copies(i):
                copy.wait_recv()
        for i in range(2):
            gc_copy(i).wait_recv()

        def column(at):
            return jnp.broadcast_to(rows_ref[at : at + 1, :], (128, 256)).T[0:192, :]

        def hot(at, width):
            wanted = column(at)
            lane = lax.broadcasted_iota(jnp.int32, (192, 128), 1)
            return jnp.concatenate(
                [jnp.where(wanted == lane + 128 * i, 1.0, 0.0).astype(BF16) for i in range(width // 128)], axis=1
            )

        first = dot(hot(0, 768), jnp.concatenate(halves(all1[...]), axis=1))
        two = jnp.concatenate(halves(all2[...]), axis=1)
        left, right = dot(hot(1, 384), two), dot(hot(2, 384), two)
        lane = lax.broadcasted_iota(jnp.int32, (192, 128), 1)
        for out, at in ((a_hi, 0), (a_lo, 128)):
            tail = left[:, at : at + 128] + 0.0
            other = pltpu.roll(right[:, at : at + 128], 64, axis=1)
            tail = jnp.where(lane < 64, tail, 0.0) + jnp.where(lane < 64, other, 0.0)
            out[...] = jnp.concatenate([first[:, at : at + 128], tail], axis=1).astype(BF16)

    def step(it, carry):
        @pl.when(it == 0)
        def _():
            make_slabs()

        mine = pl.ds(pl.multiple_of(z * 24, 8), 24)
        local = jnp.zeros((24, 128), F32)
        for f in (2, 3, 0, 1):
            ex_copy(it, mate[f]).wait_recv()
            resid = ex_src[it, face(f), :] + ex_dst[it, face(f), :] - corr[face(f), :]
            weighted = (wb[face(f), :] * resid).astype(BF16)
            wt[face(f), :] = weighted
            local = local + dot(bt_ref[:, f * FACE : (f + 1) * FACE], weighted)
        c_all[it, mine, :] = local
        for k in FAR_FIRST:
            c1_copy(it, k).start()

        @pl.when(it == 0)
        def _():
            load_n.wait()

        for f in (1, 0, 3, 2):
            up_src[it, face(f), :] = wb[face(f), :] * dot(n_ref[face(f), :], wt[...])
            up_copy(it, f).start()

        @pl.when(it == 0)
        def _():
            relay_slabs()
            make_basis()
            make_a()

        @pl.when(it > 0)
        def _():
            finish(it - 1)

        for k in range(1, 8):
            c1_copy(it, k).wait_recv()
        high, low = halves(c_all[it])
        part[it] = dot(a_hi[...], high) + dot(a_hi[...], low) + dot(a_lo[...], high)
        for k in FAR_FIRST:
            c2_copy(it, k).start()
        for f in range(4):
            up_copy(it, mate[f]).wait_recv()
            x_fine[face(f), :] = x_now[face(f), :].astype(F32) + (up_src[it, face(f), :] + up_dst[it, face(f), :])

        @pl.when(it + 1 < ITERS)
        def _():
            make_part(it + 1, x_fine[...].astype(BF16))

        total = part[it, pl.ds(pl.multiple_of(yc * 24, 8), 24), :]
        for k in range(1, 8):
            c2_copy(it, k).wait_recv()
            total = total + part_in[it, k]
        own[it, 0] = total
        for i in (2, 1, 4, 3):
            ow_copy(it, i).start()

        @pl.when(it + 1 < ITERS)
        def _():
            for i in (9, 10, 11, 12, 5, 6, 7, 8):
                ow_copy(it, i).start()
            for f in (1, 0, 3, 2):
                ex_copy(it + 1, f).start()

            @pl.when(it == 0)
            def _():
                make_t()

            for i in range(1, 13):
                ow_copy(it, i).wait_recv()
            here = five(it, 0)
            for f in range(4):
                high, low = halves(jnp.concatenate(here + five(it, 1 + f), axis=0))
                both = dot(t_hi[face(f), :], jnp.concatenate([high, low], axis=1))
                corr[face(f), :] = both[:, :128] + both[:, 128:] + dot(t_lo[face(f), :], high)

        return carry

    x_now = o_ref
    make_part(0, x_now[...])
    pl.semaphore_wait(barrier, 26)
    for k in FAR_FIRST:
        ga_copy(k).start()
    for f in (1, 0, 3, 2):
        ex_copy(0, f).start()
    for f in range(4):
        nb_copy(f).start()
    lax.fori_loop(0, ITERS, step, 0)
    for i in range(1, 5):
        ow_copy(ITERS - 1, i).wait_recv()
    finish(ITERS - 1)

    def drain(it, carry):
        for f in range(4):
            ex_copy(it, f).wait_send()
            up_copy(it, f).wait_send()
            ow_copy(it, f + 1).wait_send()
        for k in range(1, 8):
            c1_copy(it, k).wait_send()
            c2_copy(it, k).wait_send()

        @pl.when(it + 1 < ITERS)
        def _():
            for i in range(5, 13):
                ow_copy(it, i).wait_send()

        return carry

    lax.fori_loop(0, ITERS, drain, 0)
    for f in range(4):
        nb_copy(f).wait_send()
        t_copy(f).wait_send()
    for k in range(1, 8):
        ga_copy(k).wait_send()
    for i in range(6):
        for copy in gb_copies(i):
            copy.wait_send()
    for i in range(2):
        gc_copy(i).wait_send()


def shards(schur_t, neumann_t, face_weights, coarse_basis, coarse_inverse, coarse_number, loads, iterate):
    weights = face_weights.reshape(8, 128)
    basis_t = coarse_basis[0, 0].T
    vmem = pl.BlockSpec(memory_space=pltpu.VMEM)
    hbm = pl.BlockSpec(memory_space=pl.ANY)
    dma = pltpu.SemaphoreType.DMA
    out = pl.pallas_call(
        kernel,
        name="bddc_steps",
        out_shape=jax.ShapeDtypeStruct((1024, 128), BF16),
        in_specs=[hbm] * 8,
        out_specs=vmem,
        scratch_shapes=[
            pltpu.VMEM((1024, 1024), BF16),
            pltpu.VMEM((1024, 1024), BF16),
            pltpu.VMEM((8, 128), F32),
            pltpu.VMEM((24, 1024), BF16),
            pltpu.VMEM((12, 1, 768), F32),
            pltpu.VMEM((1, 1536), jnp.int32),
            pltpu.VMEM((1024, 128), BF16),
            pltpu.VMEM((1024, 128), F32),
            pltpu.VMEM((1024, 256), BF16),
            pltpu.VMEM((1024, 128), BF16),
            pltpu.VMEM((1024, 128), F32),
            pltpu.VMEM((1024, 128), F32),
            pltpu.VMEM((1024, 128), F32),
            pltpu.VMEM((1024, 128), F32),
            pltpu.VMEM((1024, 256), BF16),
            pltpu.VMEM((1024, 256), BF16),
            pltpu.VMEM((16, 768), F32),
            pltpu.VMEM((8, 256), jnp.int32),
            pltpu.VMEM((8, 8, 256), jnp.int32),
            pltpu.VMEM((8, 256), jnp.int32),
            pltpu.VMEM((8, 256), jnp.int32),
            pltpu.VMEM((ITERS, 1024, 128), F32),
            pltpu.VMEM((ITERS, 1024, 128), F32),
            pltpu.VMEM((ITERS, 1024, 128), F32),
            pltpu.VMEM((ITERS, 1024, 128), F32),
            pltpu.VMEM((ITERS, 256, 128), F32),
            pltpu.VMEM((ITERS, 192, 128), F32),
            pltpu.VMEM((ITERS, 8, 24, 128), F32),
            pltpu.VMEM((ITERS, 13, 24, 128), F32),
            pltpu.VMEM((8, 16, 256), F32),
            pltpu.VMEM((8, 16, 256), F32),
            pltpu.VMEM((96, 128), F32),
            pltpu.VMEM((48, 128), F32),
            pltpu.VMEM((768, 128), F32),
            pltpu.VMEM((384, 128), F32),
            pltpu.VMEM((192, 256), BF16),
            pltpu.VMEM((192, 256), BF16),
            pltpu.VMEM((4, 24, 256), F32),
            pltpu.VMEM((4, 24, 256), F32),
            dma((8,)),
            dma((ITERS, 4)), dma((ITERS, 4)),
            dma((ITERS, 4)), dma((ITERS, 4)),
            dma((ITERS, 8)), dma((ITERS, 8)),
            dma((ITERS, 8)), dma((ITERS, 8)),
            dma((ITERS, 13)), dma((ITERS, 13)),
            dma((8,)), dma((8,)),
            dma((2, 8)), dma((2, 8)),
            dma((4,)), dma((4,)),
            dma((4,)), dma((4,)),
        ],
        compiler_params=pltpu.CompilerParams(
            collective_id=0, has_side_effects=True, vmem_limit_bytes=67000000
        ),
    )(schur_t[0, 0], neumann_t[0, 0], weights, basis_t, coarse_inverse.reshape(12, 1, 768), coarse_number, loads[0, 0], iterate[0, 0])
    return out[None, None]


def solution(mesh):
    return jax.shard_map(
        shards,
        mesh=mesh,
        in_specs=(
            P("grp", "sub", None, None),
            P("grp", "sub", None, None),
            P("grp", "sub", None),
            P("grp", "sub", None, None),
            P("grp", "sub", None),
            P("grp", None),
            P("grp", "sub", None, None),
            P("grp", "sub", None, None),
        ),
        out_specs=P("grp", "sub", None, None),
        check_vma=False,
    )
```

```python
import jax
import jax.numpy as jnp
from jax import lax
from jax.experimental import pallas as pl
from jax.experimental.pallas import tpu as pltpu
from jax.sharding import PartitionSpec as P

ITERS = 3
FACE = 256
MESH = pl.DeviceIdType.MESH
FAR_FIRST = (4, 3, 5, 2, 6, 1, 7)
AROUND = (
    (0, 0), (0, -1), (0, 1), (-1, 0), (1, 0),
    (0, -2), (0, 2), (-2, 0), (2, 0), (-1, -1), (-1, 1), (1, -1), (1, 1),
)


def place(*steps):
    return AROUND.index((sum(a for a, _ in steps), sum(b for _, b in steps)))


FIVE = [[place(AROUND[i], AROUND[j]) for j in range(5)] for i in range(5)]
BACK = [AROUND.index((-a, -b)) for a, b in AROUND]
F32, BF16 = jnp.float32, jnp.bfloat16


def dot(a, b):
    return jnp.dot(a, b, preferred_element_type=F32)


def halves(x):
    high = x.astype(BF16)
    return high, (x - high.astype(F32)).astype(BF16)


def kernel(
    s_hbm, n_hbm, w_hbm, bt_hbm, inv_hbm, num_hbm, l_hbm, x_hbm, o_ref,
    s_ref, n_ref, w_ref, bt_ref, inv_ref, num_ref, l_ref, wb, b5, wt, x_fine, corr, t_src, t_dst, t_hi, t_lo, inv16, planes, turns, cols_ref, rows_ref,
    ex_src, ex_dst, up_src, up_dst, c_all, part, part_in, own,
    ga_src, ga_dst, slab1, slab2, all1, all2, a_hi, a_lo, nb_src, nb_dst,
    load_sem, ex_s, ex_r, up_s, up_r, c1_s, c1_r, c2_s, c2_r, ow_s, ow_r, ga_s, ga_r, gb_s, gb_r, nb_s, nb_r, t_s, t_r,
):
    g, s = lax.axis_index("grp"), lax.axis_index("sub")
    z, yc = s // 8, s % 8
    near = [(g, (s + 63) % 64), (g, (s + 1) % 64), ((g + 7) % 8, s), ((g + 1) % 8, s)]
    mate = [1, 0, 3, 2]
    around = [((g + (8 + dg)) % 8, (s + (64 + ds)) % 64) for dg, ds in AROUND[1:]]

    def z_peer(k):
        return (g, ((z + k) % 8) * 8 + yc)

    def yc_peer(k):
        return (g, z * 8 + (yc + k) % 8)

    def rc(src, dst, ssem, rsem, dev):
        return pltpu.make_async_remote_copy(
            src_ref=src, dst_ref=dst, send_sem=ssem, recv_sem=rsem, device_id=dev, device_id_type=MESH
        )

    def face(f):
        return pl.ds(f * FACE, FACE)

    def ex_copy(it, f, half):
        m = mate[f]
        here, there = pl.ds(f * FACE + half * 128, 128), pl.ds(m * FACE + half * 128, 128)
        sems = ex_s.at[it, 2 * f + half], ex_r.at[it, 2 * m + half]
        return rc(ex_src.at[it, here], ex_dst.at[it, there], *sems, near[f])

    def up_copy(it, f):
        m = mate[f]
        return rc(up_src.at[it, face(f)], up_dst.at[it, face(m)], up_s.at[it, f], up_r.at[it, m], near[f])

    def ow_copy(it, i):
        dg, ds = AROUND[i]
        there = ((g + (8 + dg)) % 8, (s + (64 + ds)) % 64)
        return rc(own.at[it, 0], own.at[it, BACK[i]], ow_s.at[it, i], ow_r.at[it, BACK[i]], there)

    def t_copy(f):
        m = mate[f]
        return rc(t_src.at[face(f)], t_dst.at[face(m)], t_s.at[f], t_r.at[m], near[f])

    def nb_copy(f):
        m = mate[f]
        return rc(nb_src.at[f], nb_dst.at[m], nb_s.at[f], nb_r.at[m], near[f])

    def c1_copy(it, k):
        mine = pl.ds(pl.multiple_of(z * 24, 8), 24)
        return rc(c_all.at[it, mine], c_all.at[it, mine], c1_s.at[it, k], c1_r.at[it, k], z_peer(k))

    def c2_copy(it, k):
        there = pl.ds(pl.multiple_of(((yc + k) % 8) * 24, 8), 24)
        return rc(part.at[it, there], part_in.at[it, k], c2_s.at[it, k], c2_r.at[it, k], yc_peer(k))

    def ga_copy(k):
        return rc(ga_src.at[(yc + k) % 8], ga_dst.at[yc], ga_s.at[k], ga_r.at[k], yc_peer(k))

    def slab_at(p, rows):
        return pl.ds(pl.multiple_of(p * rows, 8), rows)

    def gb_copies(i):
        step = (2, 6, 1, 7, 1, 7)[i]
        owner = (z + (0, 0, 0, 0, 6, 2)[i]) % 8
        there = z_peer(step)
        src1, src2 = (slab1, slab2) if i < 4 else (all1.at[slab_at(owner, 96)], all2.at[slab_at(owner, 48)])
        return [
            rc(src1, all1.at[slab_at(owner, 96)], gb_s.at[0, i], gb_r.at[0, i], there),
            rc(src2, all2.at[slab_at(owner, 48)], gb_s.at[1, i], gb_r.at[1, i], there),
        ]

    def gc_copy(i):
        every, rows = ((all1, 96), (all2, 48))[i]
        here = slab_at((z + (6, 2)[i]) % 8, rows)
        return rc(every.at[here], every.at[here], gb_s.at[i, 6], gb_r.at[i, 6], z_peer((2, 6)[i]))

    load_s, load_n, load_w, load_bt, load_inv, load_num, load_l, load_x = [
        pltpu.make_async_copy(a, b, load_sem.at[i])
        for i, (a, b) in enumerate(
            [(s_hbm, s_ref), (n_hbm, n_ref), (w_hbm, w_ref), (bt_hbm, bt_ref), (inv_hbm, inv_ref),
             (num_hbm, num_ref), (l_hbm, l_ref), (x_hbm, o_ref)]
        )
    ]
    for load in (load_num, load_inv, load_bt, load_w, load_x, load_s, load_l, load_n):
        load.start()
    c_all[...] = jnp.zeros_like(c_all)
    corr[...] = jnp.zeros_like(corr)

    barrier = pltpu.get_barrier_semaphore()
    for dev in around + [z_peer(k) for k in range(1, 8)] + [yc_peer(k) for k in range(1, 8)]:
        pl.semaphore_signal(barrier, inc=1, device_id=dev, device_id_type=MESH)

    load_num.wait()
    for q in range(8):
        at = (192 * q) // 128 * 128
        row = num_ref[:, at : at + 256]
        planes[q : q + 1, :] = row if q % 2 == 0 else pltpu.roll(row, 192, axis=1)
    for q in range(8):
        turned = planes[...] if q == 0 else pltpu.roll(planes[...], 256 - 24 * q, axis=1)
        for p in range(8):
            turns[p, q : q + 1, :] = turned[p : p + 1, :]
    lane = lax.broadcasted_iota(jnp.int32, (8, 256), 1)
    cols = jnp.where(lane < 24, turns[0], -1)
    for p in range(1, 8):
        here = (lane >= 24 * p) & (lane < 24 * p + 24)
        cols = jnp.where(here, pltpu.roll(turns[p], 24 * p, axis=1), cols)
    cols_ref[...] = cols
    n = planes[pl.ds(z, 1), :]
    zn = (n * 683) >> 16
    dn = (n * 5462) >> 16
    i, dn = n - 12 * dn, dn - 8 * zn
    r = jnp.where(i < 8, dn * 8 + i, 56 + dn * 4 + i)
    rows_ref[0:1, :] = zn * 96 + r
    rows_ref[1:2, :] = jnp.where(r < 48, zn * 48 + r, -1)
    rows_ref[2:3, :] = jnp.where(r >= 48, zn * 48 + r - 48, -1)

    load_inv.wait()
    inv16[...] = jnp.zeros_like(inv16)
    for q in range(8):
        inv16[q : q + 1, :] = inv_ref[q]
    for q in range(8, 12):
        inv16[pl.ds(q + 4 * (yc % 2), 1), :] = inv_ref[q]
    inv_hi, inv_lo = halves(inv16[...])
    pieces = jnp.concatenate([inv_hi, inv_lo], axis=0)
    order = lax.broadcasted_iota(jnp.int32, (768, 256), 0)

    def pick(q, carry):
        hot = jnp.where(order == cols_ref[pl.ds(q, 1), :], 1.0, 0.0).astype(BF16)
        both = dot(pieces, hot)
        ga_src[q] = both[:16] + both[16:]
        return carry

    lax.fori_loop(0, 8, pick, 0)
    load_bt.wait()
    basis = bt_ref[...].astype(F32)
    for f in range(4):
        nb_src[f] = basis[:, f * FACE : (f + 1) * FACE]

    ga_dst[yc] = ga_src[yc]
    load_w.wait()
    for q in range(8):
        wide = jnp.broadcast_to(w_ref[q : q + 1, :], (128, 128))
        wb[q * 128 : (q + 1) * 128, :] = wide.T

    load_x.wait()
    load_s.wait()
    load_l.wait()

    def make_part(it, current):
        for f in range(4):
            image = dot(s_ref[face(f), :], current)
            ex_src[it, face(f), :] = l_ref[face(f), :].astype(F32) - image

    def make_slabs():
        for k in range(1, 8):
            ga_copy(k).wait_recv()
        low = [ga_dst[q, 0:8, :] for q in range(8)]
        high = [ga_dst[2 * q, 8:16, :] + ga_dst[2 * q + 1, 8:16, :] for q in range(4)]
        slab = jnp.concatenate(low + high, axis=0)
        slab1[...] = slab[:, 0:128]
        slab2[...] = slab[0:48, 128:256] + pltpu.roll(slab[48:96, 128:256], 64, axis=1)
        for i in range(4):
            for copy in gb_copies(i):
                copy.start()
        all1[pl.ds(pl.multiple_of(z * 96, 8), 96), :] = slab1[...]
        all2[pl.ds(pl.multiple_of(z * 48, 8), 48), :] = slab2[...]

    def relay_slabs():
        for i in range(2):
            for copy in gb_copies(i):
                copy.wait_recv()
            for copy in gb_copies(4 + i):
                copy.start()
            gc_copy(i).start()

    def make_basis():
        for f in range(4):
            nb_copy(f).wait_recv()
        lane = lax.broadcasted_iota(jnp.int32, (128, 128), 1)
        none = jnp.zeros((24, FACE), F32)
        for f in range(4):
            rows = [nb_src[f]] + [nb_dst[f] if j == f else none for j in range(4)] + [none[:8]]
            rows = jnp.concatenate(rows, axis=0)
            for h in range(2):
                at = f * FACE + h * 128
                w = wb[at : at + 128, :]
                scaled = jnp.where(lane < 24, w, 1.0 - w) * rows[:, h * 128 : (h + 1) * 128].T
                b5[at : at + 128, :] = jnp.concatenate(halves(scaled), axis=1)
        for f in (1, 0, 3, 2):
            both = dot(s_ref[face(f), :], b5[...])
            t_src[face(f), :] = both[:, :128] + both[:, 128:]
            t_copy(f).start()

    def make_t():
        for f in range(4):
            t_copy(mate[f]).wait_recv()
            (mine_hi, mine_lo), (other_hi, other_lo) = halves(t_src[face(f), :]), halves(t_dst[face(f), :])
            t_hi[face(f), :] = jnp.concatenate([mine_hi, other_hi], axis=1)
            t_lo[face(f), :] = jnp.concatenate([mine_lo, other_lo], axis=1)

    def five(it, i):
        return [own[it, j] for j in FIVE[i]] + [jnp.zeros((8, 128), F32)]

    def finish(it):
        high, low = halves(jnp.concatenate(five(it, 0), axis=0))
        pair = jnp.concatenate([high, low], axis=1)
        for f in range(4):
            both = dot(b5[face(f), 0:128], pair)
            coarse = both[:, :128] + both[:, 128:] + dot(b5[face(f), 128:256], high)
            x_now[face(f), :] = (x_fine[face(f), :] + coarse).astype(BF16)

    def make_a():
        for i in range(2, 6):
            for copy in gb_copies(i):
                copy.wait_recv()
        for i in range(2):
            gc_copy(i).wait_recv()

        def column(at):
            return jnp.broadcast_to(rows_ref[at : at + 1, :], (128, 256)).T[0:192, :]

        def hot(at, width):
            wanted = column(at)
            lane = lax.broadcasted_iota(jnp.int32, (192, 128), 1)
            return jnp.concatenate(
                [jnp.where(wanted == lane + 128 * i, 1.0, 0.0).astype(BF16) for i in range(width // 128)], axis=1
            )

        first = dot(hot(0, 768), jnp.concatenate(halves(all1[...]), axis=1))
        two = jnp.concatenate(halves(all2[...]), axis=1)
        left, right = dot(hot(1, 384), two), dot(hot(2, 384), two)
        lane = lax.broadcasted_iota(jnp.int32, (192, 128), 1)
        for out, at in ((a_hi, 0), (a_lo, 128)):
            tail = left[:, at : at + 128] + 0.0
            other = pltpu.roll(right[:, at : at + 128], 64, axis=1)
            tail = jnp.where(lane < 64, tail, 0.0) + jnp.where(lane < 64, other, 0.0)
            out[...] = jnp.concatenate([first[:, at : at + 128], tail], axis=1).astype(BF16)

    def step(it, carry):
        @pl.when(it == 0)
        def _():
            make_slabs()

        mine = pl.ds(pl.multiple_of(z * 24, 8), 24)
        local = jnp.zeros((24, 128), F32)
        for f in (2, 3, 0, 1):
            ex_copy(it, mate[f], 0).wait_recv()
            ex_copy(it, mate[f], 1).wait_recv()
            resid = ex_src[it, face(f), :] + ex_dst[it, face(f), :] - corr[face(f), :]
            weighted = (wb[face(f), :] * resid).astype(BF16)
            wt[face(f), :] = weighted
            local = local + dot(bt_ref[:, f * FACE : (f + 1) * FACE], weighted)
        c_all[it, mine, :] = local
        for k in FAR_FIRST:
            c1_copy(it, k).start()

        @pl.when(it == 0)
        def _():
            load_n.wait()

        for f in (1, 0, 3, 2):
            up_src[it, face(f), :] = wb[face(f), :] * dot(n_ref[face(f), :], wt[...])
            up_copy(it, f).start()

        @pl.when(it == 0)
        def _():
            relay_slabs()
            make_basis()
            make_a()

        @pl.when(it > 0)
        def _():
            finish(it - 1)

        for k in range(1, 8):
            c1_copy(it, k).wait_recv()
        high, low = halves(c_all[it])
        part[it] = dot(a_hi[...], high) + dot(a_hi[...], low) + dot(a_lo[...], high)
        for k in FAR_FIRST:
            c2_copy(it, k).start()
        for f in range(4):
            up_copy(it, mate[f]).wait_recv()
            x_fine[face(f), :] = x_now[face(f), :].astype(F32) + (up_src[it, face(f), :] + up_dst[it, face(f), :])

        @pl.when(it + 1 < ITERS)
        def _():
            make_part(it + 1, x_fine[...].astype(BF16))
            for f in (1, 0, 3, 2):
                ex_copy(it + 1, f, 0).start()

        total = part[it, pl.ds(pl.multiple_of(yc * 24, 8), 24), :]
        for k in range(1, 8):
            c2_copy(it, k).wait_recv()
            total = total + part_in[it, k]
        own[it, 0] = total
        for i in (2, 1, 4, 3):
            ow_copy(it, i).start()

        @pl.when(it + 1 < ITERS)
        def _():
            for i in (9, 10, 11, 12, 5, 6, 7, 8):
                ow_copy(it, i).start()
            for f in (1, 0, 3, 2):
                ex_copy(it + 1, f, 1).start()

            @pl.when(it == 0)
            def _():
                make_t()

            for i in range(1, 13):
                ow_copy(it, i).wait_recv()
            here = five(it, 0)
            for f in range(4):
                high, low = halves(jnp.concatenate(here + five(it, 1 + f), axis=0))
                both = dot(t_hi[face(f), :], jnp.concatenate([high, low], axis=1))
                corr[face(f), :] = both[:, :128] + both[:, 128:] + dot(t_lo[face(f), :], high)

        return carry

    x_now = o_ref
    make_part(0, x_now[...])
    pl.semaphore_wait(barrier, 26)
    for k in FAR_FIRST:
        ga_copy(k).start()
    for f in range(4):
        nb_copy(f).start()
    for f in (1, 0, 3, 2):
        ex_copy(0, f, 0).start()
        ex_copy(0, f, 1).start()
    lax.fori_loop(0, ITERS, step, 0)
    for i in range(1, 5):
        ow_copy(ITERS - 1, i).wait_recv()
    finish(ITERS - 1)

    def drain(it, carry):
        for f in range(4):
            ex_copy(it, f, 0).wait_send()
            ex_copy(it, f, 1).wait_send()
            up_copy(it, f).wait_send()
            ow_copy(it, f + 1).wait_send()
        for k in range(1, 8):
            c1_copy(it, k).wait_send()
            c2_copy(it, k).wait_send()

        @pl.when(it + 1 < ITERS)
        def _():
            for i in range(5, 13):
                ow_copy(it, i).wait_send()

        return carry

    lax.fori_loop(0, ITERS, drain, 0)
    for f in range(4):
        nb_copy(f).wait_send()
        t_copy(f).wait_send()
    for k in range(1, 8):
        ga_copy(k).wait_send()
    for i in range(6):
        for copy in gb_copies(i):
            copy.wait_send()
    for i in range(2):
        gc_copy(i).wait_send()


def shards(schur_t, neumann_t, face_weights, coarse_basis, coarse_inverse, coarse_number, loads, iterate):
    weights = face_weights.reshape(8, 128)
    basis_t = coarse_basis[0, 0].T
    vmem = pl.BlockSpec(memory_space=pltpu.VMEM)
    hbm = pl.BlockSpec(memory_space=pl.ANY)
    dma = pltpu.SemaphoreType.DMA
    out = pl.pallas_call(
        kernel,
        name="bddc_steps",
        out_shape=jax.ShapeDtypeStruct((1024, 128), BF16),
        in_specs=[hbm] * 8,
        out_specs=vmem,
        scratch_shapes=[
            pltpu.VMEM((1024, 1024), BF16),
            pltpu.VMEM((1024, 1024), BF16),
            pltpu.VMEM((8, 128), F32),
            pltpu.VMEM((24, 1024), BF16),
            pltpu.VMEM((12, 1, 768), F32),
            pltpu.VMEM((1, 1536), jnp.int32),
            pltpu.VMEM((1024, 128), BF16),
            pltpu.VMEM((1024, 128), F32),
            pltpu.VMEM((1024, 256), BF16),
            pltpu.VMEM((1024, 128), BF16),
            pltpu.VMEM((1024, 128), F32),
            pltpu.VMEM((1024, 128), F32),
            pltpu.VMEM((1024, 128), F32),
            pltpu.VMEM((1024, 128), F32),
            pltpu.VMEM((1024, 256), BF16),
            pltpu.VMEM((1024, 256), BF16),
            pltpu.VMEM((16, 768), F32),
            pltpu.VMEM((8, 256), jnp.int32),
            pltpu.VMEM((8, 8, 256), jnp.int32),
            pltpu.VMEM((8, 256), jnp.int32),
            pltpu.VMEM((8, 256), jnp.int32),
            pltpu.VMEM((ITERS, 1024, 128), F32),
            pltpu.VMEM((ITERS, 1024, 128), F32),
            pltpu.VMEM((ITERS, 1024, 128), F32),
            pltpu.VMEM((ITERS, 1024, 128), F32),
            pltpu.VMEM((ITERS, 256, 128), F32),
            pltpu.VMEM((ITERS, 192, 128), F32),
            pltpu.VMEM((ITERS, 8, 24, 128), F32),
            pltpu.VMEM((ITERS, 13, 24, 128), F32),
            pltpu.VMEM((8, 16, 256), F32),
            pltpu.VMEM((8, 16, 256), F32),
            pltpu.VMEM((96, 128), F32),
            pltpu.VMEM((48, 128), F32),
            pltpu.VMEM((768, 128), F32),
            pltpu.VMEM((384, 128), F32),
            pltpu.VMEM((192, 256), BF16),
            pltpu.VMEM((192, 256), BF16),
            pltpu.VMEM((4, 24, 256), F32),
            pltpu.VMEM((4, 24, 256), F32),
            dma((8,)),
            dma((ITERS, 8)), dma((ITERS, 8)),
            dma((ITERS, 4)), dma((ITERS, 4)),
            dma((ITERS, 8)), dma((ITERS, 8)),
            dma((ITERS, 8)), dma((ITERS, 8)),
            dma((ITERS, 13)), dma((ITERS, 13)),
            dma((8,)), dma((8,)),
            dma((2, 8)), dma((2, 8)),
            dma((4,)), dma((4,)),
            dma((4,)), dma((4,)),
        ],
        compiler_params=pltpu.CompilerParams(
            collective_id=0, has_side_effects=True, vmem_limit_bytes=67000000
        ),
    )(schur_t[0, 0], neumann_t[0, 0], weights, basis_t, coarse_inverse.reshape(12, 1, 768), coarse_number, loads[0, 0], iterate[0, 0])
    return out[None, None]


def solution(mesh):
    return jax.shard_map(
        shards,
        mesh=mesh,
        in_specs=(
            P("grp", "sub", None, None),
            P("grp", "sub", None, None),
            P("grp", "sub", None),
            P("grp", "sub", None, None),
            P("grp", "sub", None),
            P("grp", None),
            P("grp", "sub", None, None),
            P("grp", "sub", None, None),
        ),
        out_specs=P("grp", "sub", None, None),
        check_vma=False,
    )
```

```python
import jax
import jax.numpy as jnp
from jax import lax
from jax.experimental import pallas as pl
from jax.experimental.pallas import tpu as pltpu
from jax.sharding import PartitionSpec as P

ITERS = 3
FACE = 256
MESH = pl.DeviceIdType.MESH
FAR_FIRST = (4, 3, 5, 2, 6, 1, 7)
AROUND = (
    (0, 0), (0, -1), (0, 1), (-1, 0), (1, 0),
    (0, -2), (0, 2), (-2, 0), (2, 0), (-1, -1), (-1, 1), (1, -1), (1, 1),
)


def place(*steps):
    return AROUND.index((sum(a for a, _ in steps), sum(b for _, b in steps)))


FIVE = [[place(AROUND[i], AROUND[j]) for j in range(5)] for i in range(5)]
BACK = [AROUND.index((-a, -b)) for a, b in AROUND]
F32, BF16 = jnp.float32, jnp.bfloat16


def dot(a, b):
    return jnp.dot(a, b, preferred_element_type=F32)


def halves(x):
    high = x.astype(BF16)
    return high, (x - high.astype(F32)).astype(BF16)


def kernel(
    s_hbm, n_hbm, w_hbm, bt_hbm, inv_hbm, num_hbm, l_hbm, x_hbm, o_ref,
    s_ref, n_ref, w_ref, bt_ref, inv_ref, num_ref, l_ref, wb, b5, wt, x_fine, corr, t_src, t_dst, t_hi, t_lo, inv16, planes, turns, cols_ref, rows_ref,
    ex_src, ex_dst, up_src, up_dst, c_all, part, part_in, own,
    ga_src, ga_dst, slab1, slab2, all1, all2, a_hi, a_lo, nb_src, nb_dst,
    load_sem, ex_s, ex_r, up_s, up_r, c1_s, c1_r, c2_s, c2_r, ow_s, ow_r, ga_s, ga_r, gb_s, gb_r, nb_s, nb_r, t_s, t_r,
):
    g, s = lax.axis_index("grp"), lax.axis_index("sub")
    z, yc = s // 8, s % 8
    near = [(g, (s + 63) % 64), (g, (s + 1) % 64), ((g + 7) % 8, s), ((g + 1) % 8, s)]
    mate = [1, 0, 3, 2]
    around = [((g + (8 + dg)) % 8, (s + (64 + ds)) % 64) for dg, ds in AROUND[1:]]

    def z_peer(k):
        return (g, ((z + k) % 8) * 8 + yc)

    def yc_peer(k):
        return (g, z * 8 + (yc + k) % 8)

    def rc(src, dst, ssem, rsem, dev):
        return pltpu.make_async_remote_copy(
            src_ref=src, dst_ref=dst, send_sem=ssem, recv_sem=rsem, device_id=dev, device_id_type=MESH
        )

    def face(f):
        return pl.ds(f * FACE, FACE)

    def ex_copy(it, f, half):
        m = mate[f]
        here, there = pl.ds(f * FACE + half * 128, 128), pl.ds(m * FACE + half * 128, 128)
        sems = ex_s.at[it, 2 * f + half], ex_r.at[it, 2 * m + half]
        return rc(ex_src.at[it, here], ex_dst.at[it, there], *sems, near[f])

    def up_copy(it, f):
        m = mate[f]
        return rc(up_src.at[it, face(f)], up_dst.at[it, face(m)], up_s.at[it, f], up_r.at[it, m], near[f])

    def ow_copy(it, i):
        dg, ds = AROUND[i]
        there = ((g + (8 + dg)) % 8, (s + (64 + ds)) % 64)
        return rc(own.at[it, 0], own.at[it, BACK[i]], ow_s.at[it, i], ow_r.at[it, BACK[i]], there)

    def t_copy(f):
        m = mate[f]
        return rc(t_src.at[face(f)], t_dst.at[face(m)], t_s.at[f], t_r.at[m], near[f])

    def nb_copy(f):
        m = mate[f]
        return rc(nb_src.at[f], nb_dst.at[m], nb_s.at[f], nb_r.at[m], near[f])

    def c1_copy(it, k):
        mine = pl.ds(pl.multiple_of(z * 24, 8), 24)
        return rc(c_all.at[it, mine], c_all.at[it, mine], c1_s.at[it, k], c1_r.at[it, k], z_peer(k))

    def c2_copy(it, k):
        there = pl.ds(pl.multiple_of(((yc + k) % 8) * 24, 8), 24)
        return rc(part.at[it, there], part_in.at[it, k], c2_s.at[it, k], c2_r.at[it, k], yc_peer(k))

    def ga_copy(k):
        return rc(ga_src.at[(yc + k) % 8], ga_dst.at[yc], ga_s.at[k], ga_r.at[k], yc_peer(k))

    def slab_at(p, rows):
        return pl.ds(pl.multiple_of(p * rows, 8), rows)

    def gb_copies(i):
        step = (2, 6, 1, 7, 1, 7)[i]
        owner = (z + (0, 0, 0, 0, 6, 2)[i]) % 8
        there = z_peer(step)
        src1, src2 = (slab1, slab2) if i < 4 else (all1.at[slab_at(owner, 96)], all2.at[slab_at(owner, 48)])
        return [
            rc(src1, all1.at[slab_at(owner, 96)], gb_s.at[0, i], gb_r.at[0, i], there),
            rc(src2, all2.at[slab_at(owner, 48)], gb_s.at[1, i], gb_r.at[1, i], there),
        ]

    def gc_copy(i):
        every, rows = ((all1, 96), (all2, 48))[i]
        here = slab_at((z + (6, 2)[i]) % 8, rows)
        return rc(every.at[here], every.at[here], gb_s.at[i, 6], gb_r.at[i, 6], z_peer((2, 6)[i]))

    load_s, load_n, load_w, load_bt, load_inv, load_num, load_l, load_x = [
        pltpu.make_async_copy(a, b, load_sem.at[i])
        for i, (a, b) in enumerate(
            [(s_hbm, s_ref), (n_hbm, n_ref), (w_hbm, w_ref), (bt_hbm, bt_ref), (inv_hbm, inv_ref),
             (num_hbm, num_ref), (l_hbm, l_ref), (x_hbm, o_ref)]
        )
    ]
    for load in (load_num, load_inv, load_x, load_s, load_l, load_bt, load_w, load_n):
        load.start()
    c_all[:, 192:256, :] = jnp.zeros((ITERS, 64, 128), F32)

    barrier = pltpu.get_barrier_semaphore()
    for dev in around + [z_peer(k) for k in range(1, 8)] + [yc_peer(k) for k in range(1, 8)]:
        pl.semaphore_signal(barrier, inc=1, device_id=dev, device_id_type=MESH)

    load_num.wait()
    for q in range(8):
        at = (192 * q) // 128 * 128
        row = num_ref[:, at : at + 256]
        planes[q : q + 1, :] = row if q % 2 == 0 else pltpu.roll(row, 192, axis=1)
    for q in range(8):
        turned = planes[...] if q == 0 else pltpu.roll(planes[...], 256 - 24 * q, axis=1)
        for p in range(8):
            turns[p, q : q + 1, :] = turned[p : p + 1, :]
    lane = lax.broadcasted_iota(jnp.int32, (8, 256), 1)
    cols = jnp.where(lane < 24, turns[0], -1)
    for p in range(1, 8):
        here = (lane >= 24 * p) & (lane < 24 * p + 24)
        cols = jnp.where(here, pltpu.roll(turns[p], 24 * p, axis=1), cols)
    cols_ref[...] = cols

    load_inv.wait()
    inv16[...] = jnp.zeros_like(inv16)
    for q in range(8):
        inv16[q : q + 1, :] = inv_ref[q]
    for q in range(8, 12):
        inv16[pl.ds(q + 4 * (yc % 2), 1), :] = inv_ref[q]
    inv_hi, inv_lo = halves(inv16[...])
    pieces = jnp.concatenate([inv_hi, inv_lo], axis=0)
    order = lax.broadcasted_iota(jnp.int32, (768, 256), 0)

    def pick(q, carry):
        hot = jnp.where(order == cols_ref[pl.ds(q, 1), :], 1.0, 0.0).astype(BF16)
        both = dot(pieces, hot)
        ga_src[q] = both[:16] + both[16:]
        return carry

    lax.fori_loop(0, 8, pick, 0)
    load_bt.wait()
    basis = bt_ref[...].astype(F32)
    for f in range(4):
        nb_src[f] = basis[:, f * FACE : (f + 1) * FACE]

    ga_dst[yc] = ga_src[yc]
    def make_part(it, current):
        for f in range(4):
            image = dot(s_ref[face(f), :], current)
            ex_src[it, face(f), :] = l_ref[face(f), :].astype(F32) - image

    def make_slabs():
        for k in range(1, 8):
            ga_copy(k).wait_recv()
        low = [ga_dst[q, 0:8, :] for q in range(8)]
        high = [ga_dst[2 * q, 8:16, :] + ga_dst[2 * q + 1, 8:16, :] for q in range(4)]
        slab = jnp.concatenate(low + high, axis=0)
        slab1[...] = slab[:, 0:128]
        slab2[...] = slab[0:48, 128:256] + pltpu.roll(slab[48:96, 128:256], 64, axis=1)
        for i in range(4):
            for copy in gb_copies(i):
                copy.start()
        all1[pl.ds(pl.multiple_of(z * 96, 8), 96), :] = slab1[...]
        all2[pl.ds(pl.multiple_of(z * 48, 8), 48), :] = slab2[...]

    def relay_slabs():
        for i in range(2):
            for copy in gb_copies(i):
                copy.wait_recv()
            for copy in gb_copies(4 + i):
                copy.start()
            gc_copy(i).start()

    def make_basis():
        for f in range(4):
            nb_copy(f).wait_recv()
        lane = lax.broadcasted_iota(jnp.int32, (128, 128), 1)
        none = jnp.zeros((24, FACE), F32)
        for f in range(4):
            rows = [nb_src[f]] + [nb_dst[f] if j == f else none for j in range(4)] + [none[:8]]
            rows = jnp.concatenate(rows, axis=0)
            for h in range(2):
                at = f * FACE + h * 128
                w = wb[at : at + 128, :]
                scaled = jnp.where(lane < 24, w, 1.0 - w) * rows[:, h * 128 : (h + 1) * 128].T
                b5[at : at + 128, :] = jnp.concatenate(halves(scaled), axis=1)
        for f in (1, 0, 3, 2):
            both = dot(s_ref[face(f), :], b5[...])
            t_src[face(f), :] = both[:, :128] + both[:, 128:]
            t_copy(f).start()

    def make_t():
        for f in range(4):
            t_copy(mate[f]).wait_recv()
            (mine_hi, mine_lo), (other_hi, other_lo) = halves(t_src[face(f), :]), halves(t_dst[face(f), :])
            t_hi[face(f), :] = jnp.concatenate([mine_hi, other_hi], axis=1)
            t_lo[face(f), :] = jnp.concatenate([mine_lo, other_lo], axis=1)

    def five(it, i):
        return [own[it, j] for j in FIVE[i]] + [jnp.zeros((8, 128), F32)]

    def finish(it):
        high, low = halves(jnp.concatenate(five(it, 0), axis=0))
        pair = jnp.concatenate([high, low], axis=1)
        for f in range(4):
            both = dot(b5[face(f), 0:128], pair)
            coarse = both[:, :128] + both[:, 128:] + dot(b5[face(f), 128:256], high)
            x_now[face(f), :] = (x_fine[face(f), :] + coarse).astype(BF16)

    def make_a():
        for i in range(2, 6):
            for copy in gb_copies(i):
                copy.wait_recv()
        for i in range(2):
            gc_copy(i).wait_recv()

        def column(at):
            return jnp.broadcast_to(rows_ref[at : at + 1, :], (128, 256)).T[0:192, :]

        def hot(at, width):
            wanted = column(at)
            lane = lax.broadcasted_iota(jnp.int32, (192, 128), 1)
            return jnp.concatenate(
                [jnp.where(wanted == lane + 128 * i, 1.0, 0.0).astype(BF16) for i in range(width // 128)], axis=1
            )

        first = dot(hot(0, 768), jnp.concatenate(halves(all1[...]), axis=1))
        two = jnp.concatenate(halves(all2[...]), axis=1)
        left, right = dot(hot(1, 384), two), dot(hot(2, 384), two)
        lane = lax.broadcasted_iota(jnp.int32, (192, 128), 1)
        for out, at in ((a_hi, 0), (a_lo, 128)):
            tail = left[:, at : at + 128] + 0.0
            other = pltpu.roll(right[:, at : at + 128], 64, axis=1)
            tail = jnp.where(lane < 64, tail, 0.0) + jnp.where(lane < 64, other, 0.0)
            out[...] = jnp.concatenate([first[:, at : at + 128], tail], axis=1).astype(BF16)

    def step(it, carry):
        @pl.when(it == 0)
        def _():
            make_slabs()

        mine = pl.ds(pl.multiple_of(z * 24, 8), 24)
        local = jnp.zeros((24, 128), F32)
        for f in (2, 3, 0, 1):
            ex_copy(it, mate[f], 0).wait_recv()
            ex_copy(it, mate[f], 1).wait_recv()
            resid = ex_src[it, face(f), :] + ex_dst[it, face(f), :] - corr[face(f), :]
            weighted = (wb[face(f), :] * resid).astype(BF16)
            wt[face(f), :] = weighted
            local = local + dot(bt_ref[:, f * FACE : (f + 1) * FACE], weighted)
        c_all[it, mine, :] = local
        for k in FAR_FIRST:
            c1_copy(it, k).start()

        @pl.when(it == 0)
        def _():
            load_n.wait()

        for f in (1, 0, 3, 2):
            up_src[it, face(f), :] = wb[face(f), :] * dot(n_ref[face(f), :], wt[...])
            up_copy(it, f).start()

        @pl.when(it == 0)
        def _():
            relay_slabs()
            make_basis()
            make_a()

        @pl.when(it > 0)
        def _():
            finish(it - 1)

        for k in range(1, 8):
            c1_copy(it, k).wait_recv()
        high, low = halves(c_all[it])
        part[it] = dot(a_hi[...], high) + dot(a_hi[...], low) + dot(a_lo[...], high)
        for k in FAR_FIRST:
            c2_copy(it, k).start()
        for f in range(4):
            up_copy(it, mate[f]).wait_recv()
            x_fine[face(f), :] = x_now[face(f), :].astype(F32) + (up_src[it, face(f), :] + up_dst[it, face(f), :])

        @pl.when(it + 1 < ITERS)
        def _():
            make_part(it + 1, x_fine[...].astype(BF16))
            for f in (1, 0, 3, 2):
                ex_copy(it + 1, f, 0).start()

        total = part[it, pl.ds(pl.multiple_of(yc * 24, 8), 24), :]
        for k in range(1, 8):
            c2_copy(it, k).wait_recv()
            total = total + part_in[it, k]
        own[it, 0] = total
        for i in (2, 1, 4, 3):
            ow_copy(it, i).start()

        @pl.when(it + 1 < ITERS)
        def _():
            for i in (9, 10, 11, 12, 5, 6, 7, 8):
                ow_copy(it, i).start()
            for f in (1, 0, 3, 2):
                ex_copy(it + 1, f, 1).start()

            @pl.when(it == 0)
            def _():
                make_t()

            for i in range(1, 13):
                ow_copy(it, i).wait_recv()
            here = five(it, 0)
            for f in range(4):
                high, low = halves(jnp.concatenate(here + five(it, 1 + f), axis=0))
                both = dot(t_hi[face(f), :], jnp.concatenate([high, low], axis=1))
                corr[face(f), :] = both[:, :128] + both[:, 128:] + dot(t_lo[face(f), :], high)

        return carry

    x_now = o_ref
    pl.semaphore_wait(barrier, 26)
    for k in FAR_FIRST:
        ga_copy(k).start()
    for f in range(4):
        nb_copy(f).start()
    load_x.wait()
    load_s.wait()
    load_l.wait()
    make_part(0, x_now[...])
    for f in (1, 0, 3, 2):
        ex_copy(0, f, 0).start()
        ex_copy(0, f, 1).start()
    n = planes[pl.ds(z, 1), :]
    zn = (n * 683) >> 16
    dn = (n * 5462) >> 16
    i, dn = n - 12 * dn, dn - 8 * zn
    r = jnp.where(i < 8, dn * 8 + i, 56 + dn * 4 + i)
    rows_ref[0:1, :] = zn * 96 + r
    rows_ref[1:2, :] = jnp.where(r < 48, zn * 48 + r, -1)
    rows_ref[2:3, :] = jnp.where(r >= 48, zn * 48 + r - 48, -1)
    load_w.wait()
    for q in range(8):
        wide = jnp.broadcast_to(w_ref[q : q + 1, :], (128, 128))
        wb[q * 128 : (q + 1) * 128, :] = wide.T
    corr[...] = jnp.zeros_like(corr)
    lax.fori_loop(0, ITERS, step, 0)
    for i in range(1, 5):
        ow_copy(ITERS - 1, i).wait_recv()
    finish(ITERS - 1)

    def drain(it, carry):
        for f in range(4):
            ex_copy(it, f, 0).wait_send()
            ex_copy(it, f, 1).wait_send()
            up_copy(it, f).wait_send()
            ow_copy(it, f + 1).wait_send()
        for k in range(1, 8):
            c1_copy(it, k).wait_send()
            c2_copy(it, k).wait_send()

        @pl.when(it + 1 < ITERS)
        def _():
            for i in range(5, 13):
                ow_copy(it, i).wait_send()

        return carry

    lax.fori_loop(0, ITERS, drain, 0)
    for f in range(4):
        nb_copy(f).wait_send()
        t_copy(f).wait_send()
    for k in range(1, 8):
        ga_copy(k).wait_send()
    for i in range(6):
        for copy in gb_copies(i):
            copy.wait_send()
    for i in range(2):
        gc_copy(i).wait_send()


def shards(schur_t, neumann_t, face_weights, coarse_basis, coarse_inverse, coarse_number, loads, iterate):
    weights = face_weights.reshape(8, 128)
    basis_t = coarse_basis[0, 0].T
    vmem = pl.BlockSpec(memory_space=pltpu.VMEM)
    hbm = pl.BlockSpec(memory_space=pl.ANY)
    dma = pltpu.SemaphoreType.DMA
    out = pl.pallas_call(
        kernel,
        name="bddc_steps",
        out_shape=jax.ShapeDtypeStruct((1024, 128), BF16),
        in_specs=[hbm] * 8,
        out_specs=vmem,
        scratch_shapes=[
            pltpu.VMEM((1024, 1024), BF16),
            pltpu.VMEM((1024, 1024), BF16),
            pltpu.VMEM((8, 128), F32),
            pltpu.VMEM((24, 1024), BF16),
            pltpu.VMEM((12, 1, 768), F32),
            pltpu.VMEM((1, 1536), jnp.int32),
            pltpu.VMEM((1024, 128), BF16),
            pltpu.VMEM((1024, 128), F32),
            pltpu.VMEM((1024, 256), BF16),
            pltpu.VMEM((1024, 128), BF16),
            pltpu.VMEM((1024, 128), F32),
            pltpu.VMEM((1024, 128), F32),
            pltpu.VMEM((1024, 128), F32),
            pltpu.VMEM((1024, 128), F32),
            pltpu.VMEM((1024, 256), BF16),
            pltpu.VMEM((1024, 256), BF16),
            pltpu.VMEM((16, 768), F32),
            pltpu.VMEM((8, 256), jnp.int32),
            pltpu.VMEM((8, 8, 256), jnp.int32),
            pltpu.VMEM((8, 256), jnp.int32),
            pltpu.VMEM((8, 256), jnp.int32),
            pltpu.VMEM((ITERS, 1024, 128), F32),
            pltpu.VMEM((ITERS, 1024, 128), F32),
            pltpu.VMEM((ITERS, 1024, 128), F32),
            pltpu.VMEM((ITERS, 1024, 128), F32),
            pltpu.VMEM((ITERS, 256, 128), F32),
            pltpu.VMEM((ITERS, 192, 128), F32),
            pltpu.VMEM((ITERS, 8, 24, 128), F32),
            pltpu.VMEM((ITERS, 13, 24, 128), F32),
            pltpu.VMEM((8, 16, 256), F32),
            pltpu.VMEM((8, 16, 256), F32),
            pltpu.VMEM((96, 128), F32),
            pltpu.VMEM((48, 128), F32),
            pltpu.VMEM((768, 128), F32),
            pltpu.VMEM((384, 128), F32),
            pltpu.VMEM((192, 256), BF16),
            pltpu.VMEM((192, 256), BF16),
            pltpu.VMEM((4, 24, 256), F32),
            pltpu.VMEM((4, 24, 256), F32),
            dma((8,)),
            dma((ITERS, 8)), dma((ITERS, 8)),
            dma((ITERS, 4)), dma((ITERS, 4)),
            dma((ITERS, 8)), dma((ITERS, 8)),
            dma((ITERS, 8)), dma((ITERS, 8)),
            dma((ITERS, 13)), dma((ITERS, 13)),
            dma((8,)), dma((8,)),
            dma((2, 8)), dma((2, 8)),
            dma((4,)), dma((4,)),
            dma((4,)), dma((4,)),
        ],
        compiler_params=pltpu.CompilerParams(
            collective_id=0, has_side_effects=True, vmem_limit_bytes=66700000
        ),
    )(schur_t[0, 0], neumann_t[0, 0], weights, basis_t, coarse_inverse.reshape(12, 1, 768), coarse_number, loads[0, 0], iterate[0, 0])
    return out[None, None]


def solution(mesh):
    return jax.shard_map(
        shards,
        mesh=mesh,
        in_specs=(
            P("grp", "sub", None, None),
            P("grp", "sub", None, None),
            P("grp", "sub", None),
            P("grp", "sub", None, None),
            P("grp", "sub", None),
            P("grp", None),
            P("grp", "sub", None, None),
            P("grp", "sub", None, None),
        ),
        out_specs=P("grp", "sub", None, None),
        check_vma=False,
    )
```
